256 devices in a mesh: seq: 32 (over z, y), head: 8 (over x, core).
Axes of the slice: x: 4, y: 4, z: 8, core: 2. Of those that a mesh axis runs over, the one named last changes fastest.
Arguments:
- hidden_states: bfloat16 [8, 5, 8192], P(None, None, 'seq'), may hold values from -6 to 6
- w_query: bfloat16 [8192, 8192], P('seq', 'head'), may hold values from -0.0625 to 0.0625
- w_key: bfloat16 [8192, 1024], P('seq', 'head'), may hold values from -0.15625 to 0.15625
- w_value: bfloat16 [8192, 1024], P('seq', 'head'), may hold values from -0.0625 to 0.0625
- w_out: bfloat16 [8192, 8192], P('head', 'seq'), may hold values from -0.0625 to 0.0625
- key_cache: bfloat16 [8, 32768, 1024], P(None, 'seq', 'head'), may hold values from -104 to 104
- value_cache: bfloat16 [8, 32768, 1024], P(None, 'seq', 'head'), may hold values from -6 to 6
- context_lengths: int32 [8], replicated, may hold values from 8192 to 32768, as said below
- keep_blocks: int32 [8, 256], P(None, 'seq'), may hold values from 0 to 1, as said below
Outputs:
- verify_out: bfloat16 [8, 5, 8192], P(None, None, 'seq')
- draft_out: bfloat16 [8, 4, 8192], P(None, None, 'seq')
The draws below stay inside these ranges and needn't reach their ends.
Inputs may be any that keep to these rules, and one draw needn't show every extreme that they name: `keep_blocks`: block 0 of every sequence is kept. `context_lengths`: one sequence has length 32768.
All inputs are finite; a program needn't handle non-finite values.
Results may differ from the reference program's by a relative error of at most 0.017.
Values may be sent and summed in bfloat16 or wider, within the bound.
No kernel may reach another device: no remote copies, remote signals or barrier semaphores. Data moves between devices by JAX's collectives and lax.ppermute only.
A program may use at most 64 MiB of HBM per device.

```python
import jax
import jax.numpy as jnp
from jax import lax

D = 8192
HEADS = 64
KV_HEADS = 8
HEAD_DIM = 128
B = 8
VERIFY = 5
BLOCK = 128
CONTEXT = 32768
DRAFT = 4
N_HEAD = 8


def draw_key_cache(key, part):
    shape_all = (B, CONTEXT, KV_HEADS * HEAD_DIM)
    values = 2.5 * jax.random.truncated_normal(key, -4.0, 4.0, shape_all, jnp.float32)
    return values.astype(jnp.bfloat16)


def draw_context_lengths(key, part):
    length_key, row_key = jax.random.split(key)
    lengths = jax.random.randint(length_key, (B,), CONTEXT // 4, CONTEXT + 1)
    full_row = jax.random.randint(row_key, (), 0, B)
    return jnp.where(jnp.arange(B) == full_row, CONTEXT, lengths).astype(jnp.int32)


def draw_keep_blocks(key, part):
    kept_flags = jax.random.randint(key, (B, CONTEXT // BLOCK), 0, 4) == 0
    first_block = jnp.arange(CONTEXT // BLOCK)[None, :] == 0
    return (kept_flags | first_block).astype(jnp.int32)


def steps_of(rng, shape, shards, smallest, largest):
    gain, own = 1.0, jax.random.fold_in(rng, 6)
    for axis_at, blocks in shards:
        draws = jnp.exp(jax.random.uniform(jax.random.fold_in(own, axis_at), (blocks,), jnp.float32, smallest / len(shards), largest / len(shards)))
        gain = gain * jnp.repeat(draws, shape[axis_at] // blocks).reshape([-1 if axis == axis_at else 1 for axis in range(len(shape))])
    return gain


def normal_values(key, extent, deviation, limit, pieces=(), kind=jnp.bfloat16):
    values = deviation * jax.random.normal(key, extent, jnp.float32)
    if pieces:
        values = values * steps_of(key, extent, pieces, -0.22, 0.18)
    return jnp.clip(values, -limit, limit).astype(kind)


def setup_inputs(seed: int = 0) -> dict:
    key_list = jax.random.split(jax.random.key(seed), 10)
    return {
        "hidden_states": normal_values(key_list[0], (B, VERIFY, D), 1.0, 6.0, ((2, 32),)),
        "w_query": normal_values(key_list[1], (D, HEADS * HEAD_DIM), D ** -0.5, 0.0625, ((0, 32), (1, 8))),
        "w_key": normal_values(key_list[2], (D, KV_HEADS * HEAD_DIM), (D // 6) ** -0.5, 0.15625, ((0, 32), (1, 8))),
        "w_value": normal_values(key_list[3], (D, KV_HEADS * HEAD_DIM), D ** -0.5, 0.0625, ((0, 32), (1, 8))),
        "w_out": normal_values(key_list[4], (HEADS * HEAD_DIM, D), (HEADS * HEAD_DIM) ** -0.5, 0.0625, ((0, 8), (1, 32))),
        "key_cache": draw_key_cache(jax.random.fold_in(key_list[9], 71), 0),
        "value_cache": normal_values(key_list[6], (B, CONTEXT, KV_HEADS * HEAD_DIM), 1.0, 6.0, ((1, 32), (2, 8))),
        "context_lengths": draw_context_lengths(jax.random.fold_in(key_list[9], 71), 0),
        "keep_blocks": draw_keep_blocks(jax.random.fold_in(key_list[9], 71), 0),
    }


big_negative = -1.0e30


def rotate(values_in, positions):
    half_dim = HEAD_DIM // 2
    inverse = 500000.0 ** (-(jnp.arange(half_dim, dtype=jnp.float32) * 2.0) / HEAD_DIM)
    angles = positions[:, :, None, None].astype(jnp.float32) * inverse
    cosine = jnp.cos(angles)
    sine = jnp.sin(angles)
    first_half = values_in[..., :half_dim]
    second_half = values_in[..., half_dim:]
    return jnp.concatenate([first_half * cosine - second_half * sine, second_half * cosine + first_half * sine], axis=-1)


def attend(scores, new_scores, cache_mask, new_mask, cache_values, new_values):
    masked = jnp.where(cache_mask[None, None, None, :], scores, big_negative)
    masked_new = jnp.where(new_mask[None, :, None, :], new_scores, big_negative)
    peak_value = jnp.maximum(jnp.max(masked, axis=-1), jnp.max(masked_new, axis=-1))
    cache_weights = jnp.where(cache_mask[None, None, None, :], jnp.exp(masked - peak_value[..., None]), 0.0)
    new_weights = jnp.where(new_mask[None, :, None, :], jnp.exp(masked_new - peak_value[..., None]), 0.0)
    total_sum = jnp.sum(cache_weights, axis=-1) + jnp.sum(new_weights, axis=-1)
    weighted = jnp.einsum("kjgt,tkd->kjgd", cache_weights.astype(jnp.bfloat16).astype(jnp.float32), cache_values.astype(jnp.float32))
    weighted = weighted + jnp.einsum("kjgi,ikd->kjgd", new_weights.astype(jnp.bfloat16).astype(jnp.float32), new_values.astype(jnp.float32))
    result = weighted / total_sum[..., None]
    return result.transpose(1, 0, 2, 3).reshape(result.shape[1], HEADS * HEAD_DIM)


def project_groups(attended, w_out):
    group_cols = HEADS * HEAD_DIM // N_HEAD
    total = jnp.zeros((attended.shape[0], D), jnp.float32)
    for group in range(N_HEAD):
        part_rows = attended[:, group * group_cols:(group + 1) * group_cols]
        part_weight = w_out[group * group_cols:(group + 1) * group_cols]
        partial_value = jnp.dot(part_rows, part_weight, preferred_element_type=jnp.float32).astype(jnp.bfloat16)
        total = total + partial_value.astype(jnp.float32)
    return total.astype(jnp.bfloat16)


def reference(hidden_states, w_query, w_key, w_value, w_out, key_cache, value_cache, context_lengths, keep_blocks):
    group_size = HEADS // KV_HEADS
    score_scale = HEAD_DIM ** -0.5
    tok_rows = hidden_states.reshape(B * VERIFY, D)
    query_raw = jnp.dot(tok_rows, w_query, preferred_element_type=jnp.float32).reshape(B, VERIFY, HEADS, HEAD_DIM)
    key_raw = jnp.dot(tok_rows, w_key, preferred_element_type=jnp.float32).reshape(B, VERIFY, KV_HEADS, HEAD_DIM)
    value_raw = jnp.dot(tok_rows, w_value, preferred_element_type=jnp.float32).reshape(B, VERIFY, KV_HEADS, HEAD_DIM)
    positions = context_lengths[:, None] + jnp.arange(VERIFY, dtype=jnp.int32)[None, :]
    query_rot = rotate(query_raw, positions).astype(jnp.bfloat16)
    key_rot = rotate(key_raw, positions).astype(jnp.bfloat16)
    new_values = value_raw.astype(jnp.bfloat16)
    key_positions = jnp.arange(CONTEXT, dtype=jnp.int32)
    causal = jnp.arange(VERIFY)[None, :] <= jnp.arange(VERIFY)[:, None]

    def one_sequence(row_items):
        query_row, key_row, value_row, cache_keys, cache_values, length, keep_row = row_items
        grouped = query_row.reshape(VERIFY, KV_HEADS, group_size, HEAD_DIM).astype(jnp.float32)
        cache_keys = cache_keys.reshape(CONTEXT, KV_HEADS, HEAD_DIM)
        cache_values = cache_values.reshape(CONTEXT, KV_HEADS, HEAD_DIM)
        scores = jnp.einsum("jkgd,tkd->kjgt", grouped, cache_keys.astype(jnp.float32)) * score_scale
        new_scores = jnp.einsum("jkgd,ikd->kjgi", grouped, key_row.astype(jnp.float32)) * score_scale
        live_mask = key_positions < length
        kept_mask = live_mask & (jnp.repeat(keep_row, BLOCK) > 0)
        target_heads = attend(scores, new_scores, live_mask, causal, cache_values, value_row)
        draft_heads = attend(scores[:, :DRAFT], new_scores[:, :DRAFT], kept_mask, causal[:DRAFT], cache_values, value_row)
        return target_heads.astype(jnp.bfloat16), draft_heads.astype(jnp.bfloat16)

    target_all, draft_all = lax.map(one_sequence, (query_rot, key_rot, new_values, key_cache, value_cache, context_lengths, keep_blocks))
    verify_out = project_groups(target_all.reshape(B * VERIFY, HEADS * HEAD_DIM), w_out)
    draft_out = project_groups(draft_all.reshape(B * DRAFT, HEADS * HEAD_DIM), w_out)
    return verify_out.reshape(B, VERIFY, D), draft_out.reshape(B, DRAFT, D)
```

```python
import jax
import jax.numpy as jnp
import numpy as np
from jax import lax
from jax.experimental import pallas as pl
from jax.experimental.pallas import tpu as pltpu
from jax.sharding import PartitionSpec as P

LANES = 128
ROWS = 8
BATCH = 8
VERIFY = 5
DRAFT = 4
TILES = VERIFY + DRAFT
SEQ = 32
HEADS = 8
TOKENS = BATCH * VERIFY
QUERY_ROWS = TOKENS * ROWS
PER_OWNER = 3
OWNERS = BATCH * TILES // PER_OWNER
MESSAGE = 16
NEGATIVE = -(2.0**100)
SCALE = LANES**-0.5
F32 = jnp.float32
BF16 = jnp.bfloat16


def project(hidden_ref, query_ref, key_ref, value_ref, out_ref, tokens, flat):
    for b in range(BATCH):
        tokens[pl.ds(b * VERIFY, VERIFY), :] = hidden_ref[b].astype(F32)
    rows = tokens[...].astype(BF16)
    query = jnp.dot(rows, query_ref[...], preferred_element_type=F32)
    for h in range(ROWS):
        flat[pl.ds(h, TOKENS, stride=ROWS), :] = query[:, h * LANES : (h + 1) * LANES]
    flat[pl.ds(QUERY_ROWS, TOKENS), :] = jnp.dot(rows, key_ref[...], preferred_element_type=F32)
    flat[pl.ds(QUERY_ROWS + TOKENS, TOKENS), :] = jnp.dot(
        rows, value_ref[...], preferred_element_type=F32
    )
    used = QUERY_ROWS + 2 * TOKENS
    flat[pl.ds(used, SEQ * MESSAGE - used), :] = jnp.zeros((SEQ * MESSAGE - used, LANES), F32)
    out_ref[...] = flat[...].reshape(SEQ, MESSAGE, LANES).astype(out_ref.dtype)


def rotate(parts_ref, cosine_ref, sine_ref, out_ref):
    total = parts_ref[0].astype(F32)
    for s in range(1, SEQ):
        total += parts_ref[s].astype(F32)
    swapped = pltpu.roll(total, LANES // 2, 1)
    rotated = (total * cosine_ref[...] + swapped * sine_ref[...]).astype(BF16)
    for s in range(SEQ):
        out_ref[s] = rotated


def split(value):
    high = value.astype(BF16).astype(F32)
    return high, (value - high).astype(BF16).astype(F32)


def attend(
    lengths_ref, keep_ref, first_ref, all_ref, key_hbm, value_hbm, out_ref, keys, values, sems
):
    def copies(b):
        return (
            pltpu.make_async_copy(key_hbm.at[b], keys.at[b], sems.at[0, b]),
            pltpu.make_async_copy(value_hbm.at[b], values.at[b], sems.at[1, b]),
        )

    for b in range(BATCH):
        for copy in copies(b):
            copy.start()
    context = keys.shape[1]
    first = first_ref[0]
    position = first + lax.broadcasted_iota(jnp.int32, (1, context), 1)
    lane = lax.broadcasted_iota(jnp.int32, (ROWS, LANES), 1)
    new_rows = lax.broadcasted_iota(jnp.int32, (QUERY_ROWS // BATCH, LANES), 0) // ROWS
    new_lanes = lax.broadcasted_iota(jnp.int32, (QUERY_ROWS // BATCH, LANES), 1)
    new_keys = jnp.concatenate(
        [all_ref[pl.ds(QUERY_ROWS, TOKENS), :], jnp.zeros((LANES - TOKENS, LANES), BF16)], axis=0
    )
    new_values = jnp.concatenate(
        [
            all_ref[pl.ds(QUERY_ROWS + TOKENS, TOKENS), :],
            jnp.zeros((LANES - TOKENS, LANES), BF16),
        ],
        axis=0,
    )
    transposed = (((1,), (1,)), ((), ()))
    for b in range(BATCH):
        for copy in copies(b):
            copy.wait()
        query = all_ref[pl.ds(b * VERIFY * ROWS, VERIFY * ROWS), :]
        scores = (
            lax.dot_general(query, keys[b], transposed, preferred_element_type=F32) * SCALE
        )
        new_scores = (
            lax.dot_general(query, new_keys, transposed, preferred_element_type=F32) * SCALE
        )
        new_at = new_lanes - b * VERIFY
        seen = (new_at >= 0) & (new_at <= new_rows) & (first == 0)
        new_scores = jnp.where(seen, new_scores, NEGATIVE)
        live = jnp.where(position < lengths_ref[b], 0.0, NEGATIVE)
        kept = jnp.concatenate(
            [
                jnp.where(
                    keep_ref[b, c] > 0, live[:, c * LANES : (c + 1) * LANES], NEGATIVE
                )
                for c in range(context // LANES)
            ],
            axis=1,
        )
        weighted, stats = [], []
        for bias, rows in ((live, VERIFY * ROWS), (kept, DRAFT * ROWS)):
            masked = scores[:rows] + bias
            masked_new = new_scores[:rows]
            peak = jnp.maximum(
                jnp.max(masked, axis=1, keepdims=True), jnp.max(masked_new, axis=1, keepdims=True)
            )
            peak_high, peak_low = split(peak)
            base = peak_high + peak_low
            weights = jnp.exp(masked - base)
            weights_new = jnp.exp(masked_new - base)
            total = jnp.sum(weights, axis=1, keepdims=True) + jnp.sum(
                weights_new, axis=1, keepdims=True
            )
            result = jnp.dot(weights.astype(BF16), values[b], preferred_element_type=F32)
            result += jnp.dot(weights_new.astype(BF16), new_values, preferred_element_type=F32)
            total_high, total_low = split(total)
            for t in range(rows // ROWS):
                at = slice(t * ROWS, (t + 1) * ROWS)
                weighted.append(result[at])
                stats.append((peak_high[at], peak_low[at], total_high[at], total_low[at]))
        for i in range(TILES // PER_OWNER):
            packed = jnp.zeros((ROWS, LANES), F32)
            for u in range(PER_OWNER):
                for k, value in enumerate(stats[i * PER_OWNER + u]):
                    packed = jnp.where(lane == 4 * u + k, value, packed)
            tiles = weighted[i * PER_OWNER : (i + 1) * PER_OWNER] + [packed]
            out_ref[b * (TILES // PER_OWNER) + i] = jnp.concatenate(tiles, axis=0).astype(BF16)
    for d in range(OWNERS, SEQ):
        out_ref[d] = jnp.zeros(out_ref.shape[1:], BF16)


def merge(parts_ref, out_ref):
    acc_rows = PER_OWNER * ROWS
    stats = []
    for s in range(SEQ):
        packed = parts_ref[s][acc_rows:].astype(F32)
        stats.append(packed + pltpu.roll(packed, LANES - 1, 1))
    peak = stats[0]
    for s in range(1, SEQ):
        peak = jnp.maximum(peak, stats[s])
    total = jnp.zeros((ROWS, LANES), F32)
    sums = [jnp.zeros((ROWS, LANES), F32) for _ in range(PER_OWNER)]
    for s in range(SEQ):
        factor = jnp.exp(stats[s] - peak)
        total += factor * pltpu.roll(stats[s], LANES - 2, 1)
        part = parts_ref[s][:acc_rows].astype(F32)
        for u in range(PER_OWNER):
            sums[u] += part[u * ROWS : (u + 1) * ROWS] * factor[:, 4 * u : 4 * u + 1]
    merged = jnp.concatenate(
        [sums[u] / total[:, 4 * u : 4 * u + 1] for u in range(PER_OWNER)], axis=0
    ).astype(BF16)
    for s in range(SEQ):
        out_ref[s] = merged


def project_out(all_ref, weight_ref, out_ref, attended):
    attended[...] = all_ref[...].astype(F32)
    total = None
    for h in range(ROWS):
        rows = attended[pl.ds(h, BATCH * TILES, stride=ROWS), :].astype(BF16)
        part = jnp.dot(
            rows, weight_ref[h * LANES : (h + 1) * LANES, :], preferred_element_type=F32
        )
        total = part if total is None else total + part
    rounded = total.astype(BF16)
    for h in range(HEADS):
        out_ref[h] = rounded


def add_groups(parts_ref, verify_ref, draft_ref, total):
    summed = parts_ref[0].astype(F32)
    for h in range(1, HEADS):
        summed += parts_ref[h].astype(F32)
    total[...] = summed
    for b in range(BATCH):
        verify_ref[b] = total[pl.ds(b * TILES, VERIFY), :].astype(BF16)
        draft_ref[b] = total[pl.ds(b * TILES + VERIFY, DRAFT), :].astype(BF16)


VMEM = pl.BlockSpec(memory_space=pltpu.VMEM)
SMEM = pl.BlockSpec(memory_space=pltpu.SMEM)
ANY = pl.BlockSpec(memory_space=pl.ANY)


def tables(seq_index, context_lengths):
    at = seq_index * MESSAGE + jnp.arange(MESSAGE, dtype=jnp.int32)
    token = jnp.where(at < QUERY_ROWS, at // ROWS, (at - QUERY_ROWS) % TOKENS)
    plain = at >= QUERY_ROWS + TOKENS
    token = jnp.minimum(token, TOKENS - 1)
    position = context_lengths[token // VERIFY] + token % VERIFY
    half = LANES // 2
    inverse = 500000.0 ** (-(jnp.arange(half, dtype=F32) * 2.0) / LANES)
    angles = position[:, None].astype(F32) * inverse
    cosine, sine = jnp.cos(angles), jnp.sin(angles)
    cosine = jnp.concatenate([cosine, cosine], axis=1)
    sine = jnp.concatenate([-sine, sine], axis=1)
    return jnp.where(plain[:, None], 1.0, cosine), jnp.where(plain[:, None], 0.0, sine)


def exchange(messages, axis):
    return lax.all_to_all(messages, axis, 0, 0, tiled=True)


def per_device(
    hidden_states,
    w_query,
    w_key,
    w_value,
    w_out,
    key_cache,
    value_cache,
    context_lengths,
    keep_blocks,
):
    seq_index = lax.axis_index("seq")
    width = hidden_states.shape[2]
    context = key_cache.shape[1]
    columns = w_out.shape[1]
    shape = jax.ShapeDtypeStruct
    parts = pl.pallas_call(
        project,
        out_shape=shape((SEQ, MESSAGE, LANES), F32),
        in_specs=[VMEM] * 4,
        out_specs=VMEM,
        scratch_shapes=[
            pltpu.VMEM((TOKENS, width), F32),
            pltpu.VMEM((SEQ * MESSAGE, LANES), F32),
        ],
        name="project",
    )(hidden_states, w_query, w_key, w_value)
    cosine, sine = tables(seq_index, context_lengths)
    parts = exchange(parts, "seq")
    rotated = pl.pallas_call(
        rotate,
        out_shape=shape((SEQ, MESSAGE, LANES), BF16),
        in_specs=[VMEM] * 3,
        out_specs=VMEM,
        name="rotate",
    )(parts, cosine, sine)
    rotated = exchange(rotated, "seq")
    first = (seq_index * context).astype(jnp.int32).reshape(1)
    partial = pl.pallas_call(
        attend,
        out_shape=shape((SEQ, (PER_OWNER + 1) * ROWS, LANES), BF16),
        in_specs=[SMEM, SMEM, SMEM, VMEM, ANY, ANY],
        out_specs=VMEM,
        scratch_shapes=[
            pltpu.VMEM((BATCH, context, LANES), BF16),
            pltpu.VMEM((BATCH, context, LANES), BF16),
            pltpu.SemaphoreType.DMA((2, BATCH)),
        ],
        name="attend",
    )(
        context_lengths,
        keep_blocks,
        first,
        rotated.reshape(SEQ * MESSAGE, LANES),
        key_cache,
        value_cache,
    )
    partial = exchange(partial, "seq")
    merged = pl.pallas_call(
        merge,
        out_shape=shape((SEQ, PER_OWNER * ROWS, LANES), BF16),
        in_specs=[VMEM],
        out_specs=VMEM,
        name="merge",
    )(partial)
    merged = exchange(merged, "seq")
    groups = pl.pallas_call(
        project_out,
        out_shape=shape((HEADS, BATCH * TILES, columns), BF16),
        in_specs=[
            pl.BlockSpec((OWNERS * PER_OWNER * ROWS, LANES), lambda i: (0, 0)),
            pl.BlockSpec(w_out.shape, lambda i: (0, 0)),
        ],
        out_specs=pl.BlockSpec((HEADS, BATCH * TILES, columns), lambda i: (0, 0, 0)),
        grid=(1,),
        scratch_shapes=[pltpu.VMEM((BATCH * TILES * ROWS, LANES), F32)],
        name="project_out",
    )(merged.reshape(SEQ * PER_OWNER * ROWS, LANES), w_out)
    groups = exchange(groups, "head")
    return pl.pallas_call(
        add_groups,
        out_shape=(
            shape((BATCH, VERIFY, columns), BF16),
            shape((BATCH, DRAFT, columns), BF16),
        ),
        in_specs=[VMEM],
        out_specs=(VMEM, VMEM),
        scratch_shapes=[pltpu.VMEM((BATCH * TILES, columns), F32)],
        name="add_groups",
    )(groups)


def solution(mesh):
    placed = (
        P(None, None, "seq"),
        P("seq", "head"),
        P("seq", "head"),
        P("seq", "head"),
        P("head", "seq"),
        P(None, "seq", "head"),
        P(None, "seq", "head"),
        P(),
        P(None, "seq"),
    )
    return jax.shard_map(
        per_device,
        mesh=mesh,
        in_specs=placed,
        out_specs=(P(None, None, "seq"), P(None, None, "seq")),
        check_vma=False,
    )
```

```python
import jax
import jax.numpy as jnp
import numpy as np
from jax import lax
from jax.experimental import pallas as pl
from jax.experimental.pallas import tpu as pltpu
from jax.sharding import PartitionSpec as P

LANES = 128
ROWS = 8
BATCH = 8
VERIFY = 5
DRAFT = 4
TILES = VERIFY + DRAFT
SEQ = 32
HEADS = 8
TOKENS = BATCH * VERIFY
QUERY_ROWS = TOKENS * ROWS
PER_OWNER = 3
OWNERS = BATCH * TILES // PER_OWNER
MESSAGE = 16
NEGATIVE = -(2.0**100)
SCALE = LANES**-0.5
LOG2E = float(np.log2(np.e))
F32 = jnp.float32
BF16 = jnp.bfloat16


def project(
    hidden_hbm, query_hbm, key_hbm, value_hbm, out_ref,
    hidden_ref, query_ref, key_ref, value_ref, flat, sems,
):
    pairs = (
        (hidden_hbm, hidden_ref),
        (query_hbm, query_ref),
        (key_hbm, key_ref),
        (value_hbm, value_ref),
    )
    loads = [
        pltpu.make_async_copy(source, target, sems.at[i])
        for i, (source, target) in enumerate(pairs)
    ]
    for load in loads:
        load.start()
    for load in loads:
        load.wait()
    rows = hidden_ref[...]
    query = jnp.dot(rows, query_ref[...], preferred_element_type=F32)
    for h in range(ROWS):
        flat[pl.ds(h, TOKENS, stride=ROWS), :] = query[:, h * LANES : (h + 1) * LANES]
    flat[pl.ds(QUERY_ROWS, TOKENS), :] = jnp.dot(rows, key_ref[...], preferred_element_type=F32)
    flat[pl.ds(QUERY_ROWS + TOKENS, TOKENS), :] = jnp.dot(
        rows, value_ref[...], preferred_element_type=F32
    )
    used = QUERY_ROWS + 2 * TOKENS
    flat[pl.ds(used, SEQ * MESSAGE - used), :] = jnp.zeros((SEQ * MESSAGE - used, LANES), F32)
    out_ref[...] = flat[...].reshape(SEQ, MESSAGE, LANES).astype(out_ref.dtype)


def rotate(parts_ref, cosine_ref, sine_ref, out_ref):
    total = parts_ref[0].astype(F32)
    for s in range(1, SEQ):
        total += parts_ref[s].astype(F32)
    swapped = pltpu.roll(total, LANES // 2, 1)
    rotated = (total * cosine_ref[...] + swapped * sine_ref[...]).astype(BF16)
    for s in range(SEQ):
        out_ref[s] = rotated


def split(value):
    high = value.astype(BF16).astype(F32)
    return high, (value - high).astype(BF16).astype(F32)


def attend(
    lengths_ref, keep_ref, first_ref, all_ref, keys, value_hbm, out_ref, scores, weights, values, sem
):
    load_values = pltpu.make_async_copy(value_hbm, values, sem)
    load_values.start()
    context = keys.shape[1]
    blocks = context // LANES
    first = first_ref[0]
    position = first + lax.broadcasted_iota(jnp.int32, (1, context), 1)
    lane = lax.broadcasted_iota(jnp.int32, (ROWS, LANES), 1)
    lane_row = lax.rem(lane, BATCH)
    padding = jnp.zeros((LANES - TOKENS, LANES), BF16)
    new_keys = jnp.concatenate([all_ref[pl.ds(QUERY_ROWS, TOKENS), :], padding], axis=0)
    new_values = jnp.concatenate([all_ref[pl.ds(QUERY_ROWS + TOKENS, TOKENS), :], padding], axis=0)
    transposed = (((1,), (1,)), ((), ()))
    exponent = SCALE * LOG2E

    def tile(j, b):
        return pl.ds((j * BATCH + b) * ROWS, ROWS)

    new_scores = (
        lax.dot_general(
            all_ref[pl.ds(0, QUERY_ROWS), :], new_keys, transposed, preferred_element_type=F32
        )
        * exponent
    )
    for b in range(BATCH):
        query = jnp.concatenate([all_ref[tile(j, b), :] for j in range(VERIFY)], axis=0)
        live = jnp.where(position < lengths_ref[b], 0.0, NEGATIVE)
        scores[b] = (
            lax.dot_general(query, keys[b], transposed, preferred_element_type=F32) * exponent
            + live
        )
    kept, fresh, bases = [], [], []
    for b in range(BATCH):
        kept.append([jnp.where(keep_ref[b, c] > 0, 0.0, NEGATIVE) for c in range(blocks)])
        rows = []
        for j in range(VERIFY):
            at = (j * BATCH + b) * ROWS
            limit = jnp.where(first == 0, (j + 1) * BATCH, 0)
            seen = (lane_row == b) & (lane < limit)
            rows.append(jnp.where(seen, new_scores[at : at + ROWS], NEGATIVE))
        rows = jnp.concatenate(rows, axis=0)
        target, draft = rows, rows[: DRAFT * ROWS]
        fresh.append(jnp.concatenate([target, draft], axis=0))
        for c in range(blocks):
            block = scores[b, :, c * LANES : (c + 1) * LANES]
            target = jnp.maximum(target, block)
            draft = jnp.maximum(draft, block[: DRAFT * ROWS] + kept[b][c])
        peak = jnp.max(jnp.concatenate([target, draft], axis=0), axis=1, keepdims=True)
        bases.append(split(peak))
    totals, fresh_weights = [], []
    for b in range(BATCH):
        base = bases[b][0] + bases[b][1]
        base_target = base[: VERIFY * ROWS]
        base_draft = base[VERIFY * ROWS :]
        new_weights = jnp.exp2(fresh[b] - base)
        fresh_weights.append(new_weights)
        sums = new_weights
        for c in range(blocks):
            at = slice(c * LANES, (c + 1) * LANES)
            block = scores[b, :, at]
            result = jnp.concatenate(
                [
                    jnp.exp2(block - base_target),
                    jnp.exp2(block[: DRAFT * ROWS] + kept[b][c] - base_draft),
                ],
                axis=0,
            )
            sums += result
            weights[b, :, at] = result.astype(BF16)
        totals.append(jnp.sum(sums, axis=1, keepdims=True))
    fresh_result = jnp.dot(
        jnp.concatenate(fresh_weights, axis=0).astype(BF16),
        new_values,
        preferred_element_type=F32,
    )
    rows = TILES * ROWS
    load_values.wait()
    for b in range(BATCH):
        result = jnp.dot(weights[b], values[b], preferred_element_type=F32)
        result += fresh_result[b * rows : (b + 1) * rows]
        stats = bases[b] + split(totals[b])
        for i in range(TILES // PER_OWNER):
            packed = jnp.zeros((ROWS, LANES), F32)
            for u in range(PER_OWNER):
                t = i * PER_OWNER + u
                for k, value in enumerate(stats):
                    packed = jnp.where(
                        lane == 4 * u + k, value[t * ROWS : (t + 1) * ROWS], packed
                    )
            part = result[i * PER_OWNER * ROWS : (i + 1) * PER_OWNER * ROWS]
            out_ref[b * (TILES // PER_OWNER) + i] = jnp.concatenate([part, packed], axis=0).astype(
                BF16
            )
    for d in range(OWNERS, SEQ):
        out_ref[d] = jnp.zeros(out_ref.shape[1:], BF16)


def merge(parts_ref, out_ref):
    acc_rows = PER_OWNER * ROWS
    stats = []
    for s in range(SEQ):
        packed = parts_ref[s][acc_rows:].astype(F32)
        stats.append(packed + pltpu.roll(packed, LANES - 1, 1))
    peak = stats[0]
    for s in range(1, SEQ):
        peak = jnp.maximum(peak, stats[s])
    total = jnp.zeros((ROWS, LANES), F32)
    sums = [jnp.zeros((ROWS, LANES), F32) for _ in range(PER_OWNER)]
    for s in range(SEQ):
        factor = jnp.exp2(stats[s] - peak)
        total += factor * pltpu.roll(stats[s], LANES - 2, 1)
        part = parts_ref[s][:acc_rows].astype(F32)
        for u in range(PER_OWNER):
            sums[u] += part[u * ROWS : (u + 1) * ROWS] * factor[:, 4 * u : 4 * u + 1]
    merged = jnp.concatenate(
        [sums[u] / total[:, 4 * u : 4 * u + 1] for u in range(PER_OWNER)], axis=0
    ).astype(BF16)
    for s in range(SEQ):
        out_ref[s] = merged


def project_out(all_ref, weight_ref, out_ref, attended):
    attended[...] = all_ref[pl.ds(0, BATCH * TILES * ROWS), :].astype(F32)
    total = None
    for h in range(ROWS):
        rows = jnp.concatenate(
            [attended[pl.ds(t * ROWS + h, BATCH, stride=TILES * ROWS), :] for t in range(TILES)],
            axis=0,
        ).astype(BF16)
        part = jnp.dot(
            rows, weight_ref[h * LANES : (h + 1) * LANES, :], preferred_element_type=F32
        )
        total = part if total is None else total + part
    rounded = total.astype(BF16)
    for h in range(HEADS):
        out_ref[h] = rounded


def add_groups(parts_ref, verify_ref, draft_ref, *halves):
    summed = parts_ref[0].astype(F32)
    for h in range(1, HEADS):
        summed += parts_ref[h].astype(F32)
    rounded = summed.astype(BF16)
    for j in range(VERIFY):
        verify_ref[j] = rounded[j * BATCH : (j + 1) * BATCH]
    for k, half in enumerate(halves):
        at = slice(k * LANES, (k + 1) * LANES)
        half[...] = summed[TOKENS:, at]
        for b in range(BATCH):
            draft_ref[b, :, at] = half[pl.ds(b, DRAFT, stride=BATCH), :].astype(BF16)


VMEM = pl.BlockSpec(memory_space=pltpu.VMEM)
SMEM = pl.BlockSpec(memory_space=pltpu.SMEM)
HBM = pl.BlockSpec(memory_space=pltpu.HBM)


def resident(array):
    return pltpu.with_memory_space_constraint(array, pltpu.VMEM)


def in_place(array):
    return pltpu.with_memory_space_constraint(array, pltpu.HBM)


def tables(seq_index, context_lengths):
    at = seq_index * MESSAGE + jnp.arange(MESSAGE, dtype=jnp.int32)
    token = jnp.where(at < QUERY_ROWS, at // ROWS, (at - QUERY_ROWS) % TOKENS)
    plain = at >= QUERY_ROWS + TOKENS
    token = jnp.minimum(token, TOKENS - 1)
    position = context_lengths[token % BATCH] + token // BATCH
    half = LANES // 2
    inverse = 500000.0 ** (-(jnp.arange(half, dtype=F32) * 2.0) / LANES)
    angles = position[:, None].astype(F32) * inverse
    cosine, sine = jnp.cos(angles), jnp.sin(angles)
    cosine = jnp.concatenate([cosine, cosine], axis=1)
    sine = jnp.concatenate([-sine, sine], axis=1)
    return jnp.where(plain[:, None], 1.0, cosine), jnp.where(plain[:, None], 0.0, sine)


def exchange(messages, axis):
    return lax.all_to_all(messages, axis, 0, 0, tiled=True)


def per_device(
    hidden_states,
    w_query,
    w_key,
    w_value,
    w_out,
    key_cache,
    value_cache,
    context_lengths,
    keep_blocks,
):
    seq_index = lax.axis_index("seq")
    width = hidden_states.shape[2]
    context = key_cache.shape[1]
    columns = w_out.shape[1]
    rows = hidden_states.transpose(1, 0, 2).reshape(TOKENS, width)
    parts = pl.pallas_call(
        project,
        out_shape=pltpu.VMEM((SEQ, MESSAGE, LANES), BF16),
        in_specs=[HBM] * 4,
        out_specs=VMEM,
        scratch_shapes=[
            pltpu.VMEM((TOKENS, width), BF16),
            pltpu.VMEM(w_query.shape, BF16),
            pltpu.VMEM(w_key.shape, BF16),
            pltpu.VMEM(w_value.shape, BF16),
            pltpu.VMEM((SEQ * MESSAGE, LANES), F32),
            pltpu.SemaphoreType.DMA((4,)),
        ],
        name="project",
        compiler_params=pltpu.CompilerParams(vmem_limit_bytes=8 << 20),
    )(*(in_place(array) for array in (rows, w_query, w_key, w_value)))
    cosine, sine = tables(seq_index, context_lengths)
    parts = exchange(parts, "seq")
    rotated = pl.pallas_call(
        rotate,
        out_shape=pltpu.VMEM((SEQ, MESSAGE, LANES), BF16),
        in_specs=[VMEM] * 3,
        out_specs=VMEM,
        name="rotate",
        compiler_params=pltpu.CompilerParams(vmem_limit_bytes=8 << 20),
    )(resident(parts), resident(cosine), resident(sine))
    rotated = exchange(rotated, "seq")
    first = (seq_index * context).astype(jnp.int32).reshape(1)
    partial = pl.pallas_call(
        attend,
        out_shape=pltpu.VMEM((SEQ, (PER_OWNER + 1) * ROWS, LANES), BF16),
        in_specs=[SMEM, SMEM, SMEM, VMEM, VMEM, HBM],
        out_specs=VMEM,
        scratch_shapes=[
            pltpu.VMEM((BATCH, VERIFY * ROWS, context), F32),
            pltpu.VMEM((BATCH, TILES * ROWS, context), BF16),
            pltpu.VMEM((BATCH, context, LANES), BF16),
            pltpu.SemaphoreType.DMA,
        ],
        name="attend",
        compiler_params=pltpu.CompilerParams(vmem_limit_bytes=16 << 20),
    )(
        context_lengths,
        keep_blocks,
        first,
        resident(rotated.reshape(SEQ * MESSAGE, LANES)),
        resident(key_cache),
        in_place(value_cache),
    )
    partial = exchange(partial, "seq")
    merged = pl.pallas_call(
        merge,
        out_shape=pltpu.VMEM((SEQ, PER_OWNER * ROWS, LANES), BF16),
        in_specs=[VMEM],
        out_specs=VMEM,
        name="merge",
        compiler_params=pltpu.CompilerParams(vmem_limit_bytes=8 << 20),
    )(resident(partial))
    merged = exchange(merged, "seq").reshape(SEQ * PER_OWNER * ROWS, LANES)
    groups = pl.pallas_call(
        project_out,
        out_shape=pltpu.VMEM((HEADS, BATCH * TILES, columns), BF16),
        in_specs=[VMEM, VMEM],
        out_specs=VMEM,
        scratch_shapes=[pltpu.VMEM((BATCH * TILES * ROWS, LANES), F32)],
        name="project_out",
        compiler_params=pltpu.CompilerParams(vmem_limit_bytes=8 << 20),
    )(resident(merged), resident(w_out))
    groups = exchange(groups, "head")
    verify_out, draft_out = pl.pallas_call(
        add_groups,
        out_shape=(
            jax.ShapeDtypeStruct((VERIFY, BATCH, columns), BF16),
            jax.ShapeDtypeStruct((BATCH, DRAFT, columns), BF16),
        ),
        in_specs=[VMEM],
        out_specs=(VMEM, VMEM),
        scratch_shapes=[pltpu.VMEM((DRAFT * BATCH, LANES), F32)] * (columns // LANES),
        name="add_groups",
        compiler_params=pltpu.CompilerParams(vmem_limit_bytes=8 << 20),
    )(resident(groups))
    return verify_out.transpose(1, 0, 2), draft_out


def solution(mesh):
    placed = (
        P(None, None, "seq"),
        P("seq", "head"),
        P("seq", "head"),
        P("seq", "head"),
        P("head", "seq"),
        P(None, "seq", "head"),
        P(None, "seq", "head"),
        P(),
        P(None, "seq"),
    )
    return jax.shard_map(
        per_device,
        mesh=mesh,
        in_specs=placed,
        out_specs=(P(None, None, "seq"), P(None, None, "seq")),
        check_vma=False,
    )
```

```python
import jax
import jax.numpy as jnp
import numpy as np
from jax import lax
from jax.experimental import pallas as pl
from jax.experimental.pallas import tpu as pltpu
from jax.sharding import PartitionSpec as P

LANES = 128
ROWS = 8
BATCH = 8
VERIFY = 5
DRAFT = 4
TILES = VERIFY + DRAFT
SEQ = 32
HEADS = 8
TOKENS = BATCH * VERIFY
QUERY_ROWS = TOKENS * ROWS
PER_OWNER = 3
OWNERS = BATCH * TILES // PER_OWNER
MESSAGE = 16
NEGATIVE = -(2.0**100)
SCALE = LANES**-0.5
LOG2E = float(np.log2(np.e))
F32 = jnp.float32
BF16 = jnp.bfloat16


def project(
    hidden_hbm, query_hbm, key_hbm, value_hbm, lengths_hbm, keep_hbm, inverse_hbm,
    out_ref, cosine_ref, sine_ref, live_ref, kept_ref, fresh_ref,
    hidden_ref, query_ref, key_ref, value_ref, lengths_ref, keep_ref, inverse_ref, flat, sems,
):
    pairs = (
        (lengths_hbm, lengths_ref),
        (keep_hbm, keep_ref),
        (inverse_hbm, inverse_ref),
        (hidden_hbm, hidden_ref),
        (query_hbm, query_ref),
        (key_hbm, key_ref),
        (value_hbm, value_ref),
    )
    loads = [
        pltpu.make_async_copy(source, target, sems.at[i])
        for i, (source, target) in enumerate(pairs)
    ]
    for load in loads:
        load.start()
    for load in loads[:3]:
        load.wait()
    here = lax.axis_index("seq")
    row = lax.broadcasted_iota(jnp.int32, (ROWS, LANES), 0)
    lane = lax.broadcasted_iota(jnp.int32, (ROWS, LANES), 1)
    lengths = jnp.zeros((ROWS, LANES), jnp.int32)
    for b in range(BATCH):
        lengths = jnp.where(row == b, lengths_ref[b], lengths)
    for half in range(MESSAGE // ROWS):
        tile = here * (MESSAGE // ROWS) + half
        is_query = tile < TOKENS
        token = jnp.where(is_query, tile, 0)
        query_position = lengths_ref[lax.rem(token, BATCH)] + token // BATCH
        position = jnp.where(is_query, query_position, lengths + (tile - TOKENS))
        angle = position.astype(F32) * inverse_ref[...]
        plain = tile >= TOKENS + VERIFY
        at = slice(half * ROWS, (half + 1) * ROWS)
        sine = jnp.sin(angle)
        cosine_ref[at, :] = jnp.where(plain, 1.0, jnp.cos(angle))
        sine_ref[at, :] = jnp.where(plain, 0.0, jnp.where(lane < LANES // 2, -sine, sine))
    blocks = live_ref.shape[1] // LANES
    for c in range(blocks):
        at = slice(c * LANES, (c + 1) * LANES)
        live = jnp.where((here * blocks + c) * LANES + lane < lengths, 0.0, NEGATIVE)
        live_ref[:, at] = live
        keep = jnp.zeros((ROWS, LANES), jnp.int32)
        for b in range(BATCH):
            keep = jnp.where(row == b, keep_ref[b, c], keep)
        kept_ref[:, at] = jnp.where(keep > 0, 0.0, NEGATIVE)
    fresh_ref[...] = jnp.full((ROWS, LANES), jnp.where(here == 0, 0.0, NEGATIVE))
    for load in loads[3:]:
        load.wait()
    rows = hidden_ref[...]
    query = jnp.dot(rows, query_ref[...], preferred_element_type=F32)
    for h in range(ROWS):
        flat[pl.ds(h, TOKENS, stride=ROWS), :] = query[:, h * LANES : (h + 1) * LANES]
    flat[pl.ds(QUERY_ROWS, TOKENS), :] = jnp.dot(rows, key_ref[...], preferred_element_type=F32)
    flat[pl.ds(QUERY_ROWS + TOKENS, TOKENS), :] = jnp.dot(
        rows, value_ref[...], preferred_element_type=F32
    )
    used = QUERY_ROWS + 2 * TOKENS
    flat[pl.ds(used, SEQ * MESSAGE - used), :] = jnp.zeros((SEQ * MESSAGE - used, LANES), F32)
    out_ref[...] = flat[...].reshape(SEQ, MESSAGE, LANES).astype(out_ref.dtype)


def rotate(parts_ref, cosine_ref, sine_ref, out_ref):
    total = parts_ref[0].astype(F32)
    for s in range(1, SEQ):
        total += parts_ref[s].astype(F32)
    swapped = pltpu.roll(total, LANES // 2, 1)
    rotated = (total * cosine_ref[...] + swapped * sine_ref[...]).astype(BF16)
    for s in range(SEQ):
        out_ref[s] = rotated


def split(value):
    high = value.astype(BF16).astype(F32)
    return high, (value - high).astype(BF16).astype(F32)


def attend(
    live_ref, kept_ref, fresh_ref, all_ref, keys, values, out_ref, scores, weights
):
    blocks = keys.shape[1] // LANES
    lane = lax.broadcasted_iota(jnp.int32, (ROWS, LANES), 1)
    lane_row = lax.rem(lane, BATCH)
    padding = jnp.zeros((LANES - TOKENS, LANES), BF16)
    new_keys = jnp.concatenate([all_ref[pl.ds(QUERY_ROWS, TOKENS), :], padding], axis=0)
    new_values = jnp.concatenate([all_ref[pl.ds(QUERY_ROWS + TOKENS, TOKENS), :], padding], axis=0)
    transposed = (((1,), (1,)), ((), ()))
    exponent = SCALE * LOG2E

    def tile(j, b):
        return pl.ds((j * BATCH + b) * ROWS, ROWS)

    new_scores = (
        lax.dot_general(
            all_ref[pl.ds(0, QUERY_ROWS), :], new_keys, transposed, preferred_element_type=F32
        )
        * exponent
    )
    for b in range(BATCH):
        query = jnp.concatenate([all_ref[tile(j, b), :] for j in range(VERIFY)], axis=0)
        scores[b] = (
            lax.dot_general(query, keys[b], transposed, preferred_element_type=F32) * exponent
            + live_ref[b : b + 1, :]
        )
    kept, fresh, bases = [], [], []
    for b in range(BATCH):
        kept.append([kept_ref[b : b + 1, c * LANES : (c + 1) * LANES] for c in range(blocks)])
        rows = []
        for j in range(VERIFY):
            at = (j * BATCH + b) * ROWS
            seen = (lane_row == b) & (lane < (j + 1) * BATCH)
            rows.append(jnp.where(seen, new_scores[at : at + ROWS] + fresh_ref[...], NEGATIVE))
        rows = jnp.concatenate(rows, axis=0)
        target, draft = rows, rows[: DRAFT * ROWS]
        fresh.append(jnp.concatenate([target, draft], axis=0))
        for c in range(blocks):
            block = scores[b, :, c * LANES : (c + 1) * LANES]
            target = jnp.maximum(target, block)
            draft = jnp.maximum(draft, block[: DRAFT * ROWS] + kept[b][c])
        peak = jnp.max(jnp.concatenate([target, draft], axis=0), axis=1, keepdims=True)
        bases.append(split(peak))
    totals, fresh_weights = [], []
    for b in range(BATCH):
        base = bases[b][0] + bases[b][1]
        base_target = base[: VERIFY * ROWS]
        base_draft = base[VERIFY * ROWS :]
        new_weights = jnp.exp2(fresh[b] - base)
        fresh_weights.append(new_weights)
        sums = new_weights
        for c in range(blocks):
            at = slice(c * LANES, (c + 1) * LANES)
            block = scores[b, :, at]
            result = jnp.concatenate(
                [
                    jnp.exp2(block - base_target),
                    jnp.exp2(block[: DRAFT * ROWS] + kept[b][c] - base_draft),
                ],
                axis=0,
            )
            sums += result
            weights[b, :, at] = result.astype(BF16)
        totals.append(jnp.sum(sums, axis=1, keepdims=True))
    fresh_result = jnp.dot(
        jnp.concatenate(fresh_weights, axis=0).astype(BF16),
        new_values,
        preferred_element_type=F32,
    )
    rows = TILES * ROWS
    for b in range(BATCH):
        result = jnp.dot(weights[b], values[b], preferred_element_type=F32)
        result += fresh_result[b * rows : (b + 1) * rows]
        stats = bases[b] + split(totals[b])
        for i in range(TILES // PER_OWNER):
            packed = jnp.zeros((ROWS, LANES), F32)
            for u in range(PER_OWNER):
                t = i * PER_OWNER + u
                for k, value in enumerate(stats):
                    packed = jnp.where(
                        lane == 4 * u + k, value[t * ROWS : (t + 1) * ROWS], packed
                    )
            part = result[i * PER_OWNER * ROWS : (i + 1) * PER_OWNER * ROWS]
            out_ref[b * (TILES // PER_OWNER) + i] = jnp.concatenate([part, packed], axis=0).astype(
                BF16
            )
    for d in range(OWNERS, SEQ):
        out_ref[d] = jnp.zeros(out_ref.shape[1:], BF16)


def merge(parts_ref, out_ref):
    acc_rows = PER_OWNER * ROWS
    stats = []
    for s in range(SEQ):
        packed = parts_ref[s][acc_rows:].astype(F32)
        stats.append(packed + pltpu.roll(packed, LANES - 1, 1))
    peak = stats[0]
    for s in range(1, SEQ):
        peak = jnp.maximum(peak, stats[s])
    total = jnp.zeros((ROWS, LANES), F32)
    sums = [jnp.zeros((ROWS, LANES), F32) for _ in range(PER_OWNER)]
    for s in range(SEQ):
        factor = jnp.exp2(stats[s] - peak)
        total += factor * pltpu.roll(stats[s], LANES - 2, 1)
        part = parts_ref[s][:acc_rows].astype(F32)
        for u in range(PER_OWNER):
            sums[u] += part[u * ROWS : (u + 1) * ROWS] * factor[:, 4 * u : 4 * u + 1]
    merged = jnp.concatenate(
        [sums[u] / total[:, 4 * u : 4 * u + 1] for u in range(PER_OWNER)], axis=0
    ).astype(BF16)
    for s in range(SEQ):
        out_ref[s] = merged


def project_out(all_ref, weight_ref, out_ref, attended):
    attended[...] = all_ref[pl.ds(0, BATCH * TILES * ROWS), :].astype(F32)
    total = None
    for h in range(ROWS):
        rows = jnp.concatenate(
            [attended[pl.ds(t * ROWS + h, BATCH, stride=TILES * ROWS), :] for t in range(TILES)],
            axis=0,
        ).astype(BF16)
        part = jnp.dot(
            rows, weight_ref[h * LANES : (h + 1) * LANES, :], preferred_element_type=F32
        )
        total = part if total is None else total + part
    rounded = total.astype(BF16)
    for h in range(HEADS):
        out_ref[h] = rounded


def add_groups(parts_ref, verify_ref, draft_ref, *halves):
    summed = parts_ref[0].astype(F32)
    for h in range(1, HEADS):
        summed += parts_ref[h].astype(F32)
    rounded = summed.astype(BF16)
    for j in range(VERIFY):
        verify_ref[j] = rounded[j * BATCH : (j + 1) * BATCH]
    for k, half in enumerate(halves):
        at = slice(k * LANES, (k + 1) * LANES)
        half[...] = summed[TOKENS:, at]
        for b in range(BATCH):
            draft_ref[b, :, at] = half[pl.ds(b, DRAFT, stride=BATCH), :].astype(BF16)


VMEM = pl.BlockSpec(memory_space=pltpu.VMEM)
HBM = pl.BlockSpec(memory_space=pltpu.HBM)


def resident(array):
    return pltpu.with_memory_space_constraint(array, pltpu.VMEM)


def in_place(array):
    return pltpu.with_memory_space_constraint(array, pltpu.HBM)


def exchange(messages, axis):
    return lax.all_to_all(messages, axis, 0, 0, tiled=True)


def per_device(
    hidden_states,
    w_query,
    w_key,
    w_value,
    w_out,
    key_cache,
    value_cache,
    context_lengths,
    keep_blocks,
):
    width = hidden_states.shape[2]
    context = key_cache.shape[1]
    columns = w_out.shape[1]
    rows = hidden_states.transpose(1, 0, 2).reshape(TOKENS, width)
    half = LANES // 2
    inverse = (500000.0 ** (-(np.arange(LANES) % half) * 2.0 / LANES)).astype(np.float32)
    array = pltpu.VMEM
    parts, cosine, sine, live, kept, fresh = pl.pallas_call(
        project,
        out_shape=(
            array((SEQ, MESSAGE, LANES), BF16),
            array((MESSAGE, LANES), F32),
            array((MESSAGE, LANES), F32),
            array((BATCH, context), F32),
            array((BATCH, context), F32),
            array((ROWS, LANES), F32),
        ),
        in_specs=[HBM] * 7,
        out_specs=(VMEM,) * 6,
        scratch_shapes=[
            pltpu.VMEM((TOKENS, width), BF16),
            pltpu.VMEM(w_query.shape, BF16),
            pltpu.VMEM(w_key.shape, BF16),
            pltpu.VMEM(w_value.shape, BF16),
            pltpu.SMEM(context_lengths.shape, jnp.int32),
            pltpu.SMEM(keep_blocks.shape, jnp.int32),
            pltpu.VMEM((1, LANES), F32),
            pltpu.VMEM((SEQ * MESSAGE, LANES), F32),
            pltpu.SemaphoreType.DMA((7,)),
        ],
        name="project",
        compiler_params=pltpu.CompilerParams(vmem_limit_bytes=8 << 20),
    )(
        *(
            in_place(operand)
            for operand in (
                rows, w_query, w_key, w_value, context_lengths, keep_blocks,
                jnp.asarray(inverse).reshape(1, LANES),
            )
        )
    )
    parts = exchange(parts, "seq")
    rotated = pl.pallas_call(
        rotate,
        out_shape=pltpu.VMEM((SEQ, MESSAGE, LANES), BF16),
        in_specs=[VMEM] * 3,
        out_specs=VMEM,
        name="rotate",
        cost_estimate=pl.CostEstimate(
            flops=1000000000, transcendentals=0, bytes_accessed=64000000
        ),
        compiler_params=pltpu.CompilerParams(vmem_limit_bytes=8 << 20),
    )(resident(parts), resident(cosine), resident(sine))
    rotated = exchange(rotated, "seq")
    partial = pl.pallas_call(
        attend,
        out_shape=pltpu.VMEM((SEQ, (PER_OWNER + 1) * ROWS, LANES), BF16),
        in_specs=[VMEM] * 6,
        out_specs=VMEM,
        scratch_shapes=[
            pltpu.VMEM((BATCH, VERIFY * ROWS, context), F32),
            pltpu.VMEM((BATCH, TILES * ROWS, context), BF16),
        ],
        name="attend",
        compiler_params=pltpu.CompilerParams(vmem_limit_bytes=16 << 20),
    )(
        resident(live),
        resident(kept),
        resident(fresh),
        resident(rotated.reshape(SEQ * MESSAGE, LANES)),
        resident(key_cache),
        resident(value_cache),
    )
    partial = exchange(partial, "seq")
    merged = pl.pallas_call(
        merge,
        out_shape=pltpu.VMEM((SEQ, PER_OWNER * ROWS, LANES), BF16),
        in_specs=[VMEM],
        out_specs=VMEM,
        name="merge",
        compiler_params=pltpu.CompilerParams(vmem_limit_bytes=8 << 20),
    )(resident(partial))
    merged = exchange(merged, "seq").reshape(SEQ * PER_OWNER * ROWS, LANES)
    groups = pl.pallas_call(
        project_out,
        out_shape=pltpu.VMEM((HEADS, BATCH * TILES, columns), BF16),
        in_specs=[VMEM, VMEM],
        out_specs=VMEM,
        scratch_shapes=[pltpu.VMEM((BATCH * TILES * ROWS, LANES), F32)],
        name="project_out",
        compiler_params=pltpu.CompilerParams(vmem_limit_bytes=8 << 20),
    )(resident(merged), resident(w_out))
    groups = exchange(groups, "head")
    verify_out, draft_out = pl.pallas_call(
        add_groups,
        out_shape=(
            jax.ShapeDtypeStruct((VERIFY, BATCH, columns), BF16),
            jax.ShapeDtypeStruct((BATCH, DRAFT, columns), BF16),
        ),
        in_specs=[VMEM],
        out_specs=(VMEM, VMEM),
        scratch_shapes=[pltpu.VMEM((DRAFT * BATCH, LANES), F32)] * (columns // LANES),
        name="add_groups",
        compiler_params=pltpu.CompilerParams(vmem_limit_bytes=8 << 20),
    )(resident(groups))
    return verify_out.transpose(1, 0, 2), draft_out


def solution(mesh):
    placed = (
        P(None, None, "seq"),
        P("seq", "head"),
        P("seq", "head"),
        P("seq", "head"),
        P("head", "seq"),
        P(None, "seq", "head"),
        P(None, "seq", "head"),
        P(),
        P(None, "seq"),
    )
    return jax.shard_map(
        per_device,
        mesh=mesh,
        in_specs=placed,
        out_specs=(P(None, None, "seq"), P(None, None, "seq")),
        check_vma=False,
    )
```

```python
import jax
import jax.numpy as jnp
import numpy as np
from jax import lax
from jax.experimental import pallas as pl
from jax.experimental.pallas import tpu as pltpu
from jax.sharding import PartitionSpec as P

LANES = 128
ROWS = 8
BATCH = 8
VERIFY = 5
DRAFT = 4
TILES = VERIFY + DRAFT
SEQ = 32
HEADS = 8
CORES = 2
CHIPS = HEADS // CORES
TOKENS = BATCH * VERIFY
QUERY_ROWS = TOKENS * ROWS
PER_OWNER = 3
OWNERS = BATCH * TILES // PER_OWNER
MESSAGE = 16
NEGATIVE = -(2.0**100)
SCALE = LANES**-0.5
LOG2E = float(np.log2(np.e))
F32 = jnp.float32
BF16 = jnp.bfloat16


def project(
    hidden_hbm, query_hbm, key_hbm, value_hbm, lengths_hbm, keep_hbm, inverse_hbm,
    out_ref, cosine_ref, sine_ref, live_ref, kept_ref, fresh_ref,
    hidden_ref, query_ref, key_ref, value_ref, lengths_ref, keep_ref, inverse_ref, flat, sems,
):
    pairs = (
        (lengths_hbm, lengths_ref),
        (keep_hbm, keep_ref),
        (inverse_hbm, inverse_ref),
        (hidden_hbm, hidden_ref),
        (query_hbm, query_ref),
        (key_hbm, key_ref),
        (value_hbm, value_ref),
    )
    loads = [
        pltpu.make_async_copy(source, target, sems.at[i])
        for i, (source, target) in enumerate(pairs)
    ]
    for load in loads:
        load.start()
    for load in loads[:3]:
        load.wait()
    here = lax.axis_index("seq")
    row = lax.broadcasted_iota(jnp.int32, (ROWS, LANES), 0)
    lane = lax.broadcasted_iota(jnp.int32, (ROWS, LANES), 1)
    lengths = jnp.zeros((ROWS, LANES), jnp.int32)
    for b in range(BATCH):
        lengths = jnp.where(row == b, lengths_ref[b], lengths)
    for half in range(MESSAGE // ROWS):
        tile = here * (MESSAGE // ROWS) + half
        is_query = tile < TOKENS
        token = jnp.where(is_query, tile, 0)
        query_position = lengths_ref[lax.rem(token, BATCH)] + token // BATCH
        position = jnp.where(is_query, query_position, lengths + (tile - TOKENS))
        angle = position.astype(F32) * inverse_ref[...]
        plain = tile >= TOKENS + VERIFY
        at = slice(half * ROWS, (half + 1) * ROWS)
        sine = jnp.sin(angle)
        cosine_ref[at, :] = jnp.where(plain, 1.0, jnp.cos(angle))
        sine_ref[at, :] = jnp.where(plain, 0.0, jnp.where(lane < LANES // 2, -sine, sine))
    blocks = live_ref.shape[1] // LANES
    for c in range(blocks):
        at = slice(c * LANES, (c + 1) * LANES)
        live = jnp.where((here * blocks + c) * LANES + lane < lengths, 0.0, NEGATIVE)
        live_ref[:, at] = live
        keep = jnp.zeros((ROWS, LANES), jnp.int32)
        for b in range(BATCH):
            keep = jnp.where(row == b, keep_ref[b, c], keep)
        kept_ref[:, at] = jnp.where(keep > 0, 0.0, NEGATIVE)
    fresh_ref[...] = jnp.full((ROWS, LANES), jnp.where(here == 0, 0.0, NEGATIVE))
    for load in loads[3:]:
        load.wait()
    rows = hidden_ref[...]
    query = jnp.dot(rows, query_ref[...], preferred_element_type=F32)
    for h in range(ROWS):
        flat[pl.ds(h, TOKENS, stride=ROWS), :] = query[:, h * LANES : (h + 1) * LANES]
    flat[pl.ds(QUERY_ROWS, TOKENS), :] = jnp.dot(rows, key_ref[...], preferred_element_type=F32)
    flat[pl.ds(QUERY_ROWS + TOKENS, TOKENS), :] = jnp.dot(
        rows, value_ref[...], preferred_element_type=F32
    )
    used = QUERY_ROWS + 2 * TOKENS
    flat[pl.ds(used, SEQ * MESSAGE - used), :] = jnp.zeros((SEQ * MESSAGE - used, LANES), F32)
    out_ref[...] = flat[...].reshape(SEQ, MESSAGE, LANES).astype(out_ref.dtype)


def rotate(parts_ref, cosine_ref, sine_ref, out_ref):
    total = parts_ref[0].astype(F32)
    for s in range(1, SEQ):
        total += parts_ref[s].astype(F32)
    swapped = pltpu.roll(total, LANES // 2, 1)
    rotated = (total * cosine_ref[...] + swapped * sine_ref[...]).astype(BF16)
    for s in range(SEQ):
        out_ref[s] = rotated


def split(value):
    high = value.astype(BF16).astype(F32)
    return high, (value - high).astype(BF16).astype(F32)


def attend(
    live_ref, kept_ref, fresh_ref, all_ref, keys, values, out_ref, scores, weights
):
    blocks = keys.shape[1] // LANES
    lane = lax.broadcasted_iota(jnp.int32, (ROWS, LANES), 1)
    lane_row = lax.rem(lane, BATCH)
    padding = jnp.zeros((LANES - TOKENS, LANES), BF16)
    new_keys = jnp.concatenate([all_ref[pl.ds(QUERY_ROWS, TOKENS), :], padding], axis=0)
    new_values = jnp.concatenate([all_ref[pl.ds(QUERY_ROWS + TOKENS, TOKENS), :], padding], axis=0)
    transposed = (((1,), (1,)), ((), ()))
    exponent = SCALE * LOG2E

    def tile(j, b):
        return pl.ds((j * BATCH + b) * ROWS, ROWS)

    new_scores = (
        lax.dot_general(
            all_ref[pl.ds(0, QUERY_ROWS), :], new_keys, transposed, preferred_element_type=F32
        )
        * exponent
    )
    for b in range(BATCH):
        query = jnp.concatenate([all_ref[tile(j, b), :] for j in range(VERIFY)], axis=0)
        scores[b] = (
            lax.dot_general(query, keys[b], transposed, preferred_element_type=F32) * exponent
            + live_ref[b : b + 1, :]
        )
    kept, fresh, bases = [], [], []
    for b in range(BATCH):
        kept.append([kept_ref[b : b + 1, c * LANES : (c + 1) * LANES] for c in range(blocks)])
        rows = []
        for j in range(VERIFY):
            at = (j * BATCH + b) * ROWS
            seen = (lane_row == b) & (lane < (j + 1) * BATCH)
            rows.append(jnp.where(seen, new_scores[at : at + ROWS] + fresh_ref[...], NEGATIVE))
        rows = jnp.concatenate(rows, axis=0)
        target, draft = rows, rows[: DRAFT * ROWS]
        fresh.append(jnp.concatenate([target, draft], axis=0))
        for c in range(blocks):
            block = scores[b, :, c * LANES : (c + 1) * LANES]
            target = jnp.maximum(target, block)
            draft = jnp.maximum(draft, block[: DRAFT * ROWS] + kept[b][c])
        peak = jnp.max(jnp.concatenate([target, draft], axis=0), axis=1, keepdims=True)
        bases.append(split(peak))
    totals, fresh_weights = [], []
    for b in range(BATCH):
        base = bases[b][0] + bases[b][1]
        base_target = base[: VERIFY * ROWS]
        base_draft = base[VERIFY * ROWS :]
        new_weights = jnp.exp2(fresh[b] - base)
        fresh_weights.append(new_weights)
        sums = new_weights
        for c in range(blocks):
            at = slice(c * LANES, (c + 1) * LANES)
            block = scores[b, :, at]
            result = jnp.concatenate(
                [
                    jnp.exp2(block - base_target),
                    jnp.exp2(block[: DRAFT * ROWS] + kept[b][c] - base_draft),
                ],
                axis=0,
            )
            sums += result
            weights[b, :, at] = result.astype(BF16)
        totals.append(jnp.sum(sums, axis=1, keepdims=True))
    fresh_result = jnp.dot(
        jnp.concatenate(fresh_weights, axis=0).astype(BF16),
        new_values,
        preferred_element_type=F32,
    )
    rows = TILES * ROWS
    for b in range(BATCH):
        result = jnp.dot(weights[b], values[b], preferred_element_type=F32)
        result += fresh_result[b * rows : (b + 1) * rows]
        stats = bases[b] + split(totals[b])
        for i in range(TILES // PER_OWNER):
            packed = jnp.zeros((ROWS, LANES), F32)
            for u in range(PER_OWNER):
                t = i * PER_OWNER + u
                for k, value in enumerate(stats):
                    packed = jnp.where(
                        lane == 4 * u + k, value[t * ROWS : (t + 1) * ROWS], packed
                    )
            part = result[i * PER_OWNER * ROWS : (i + 1) * PER_OWNER * ROWS]
            out_ref[b * (TILES // PER_OWNER) + i] = jnp.concatenate([part, packed], axis=0).astype(
                BF16
            )
    for d in range(OWNERS, SEQ):
        out_ref[d] = jnp.zeros(out_ref.shape[1:], BF16)


def merge(parts_ref, out_ref):
    acc_rows = PER_OWNER * ROWS
    stats = []
    for s in range(SEQ):
        packed = parts_ref[s][acc_rows:].astype(F32)
        stats.append(packed + pltpu.roll(packed, LANES - 1, 1))
    peak = stats[0]
    for s in range(1, SEQ):
        peak = jnp.maximum(peak, stats[s])
    total = jnp.zeros((ROWS, LANES), F32)
    sums = [jnp.zeros((ROWS, LANES), F32) for _ in range(PER_OWNER)]
    for s in range(SEQ):
        factor = jnp.exp2(stats[s] - peak)
        total += factor * pltpu.roll(stats[s], LANES - 2, 1)
        part = parts_ref[s][:acc_rows].astype(F32)
        for u in range(PER_OWNER):
            sums[u] += part[u * ROWS : (u + 1) * ROWS] * factor[:, 4 * u : 4 * u + 1]
    merged = jnp.concatenate(
        [sums[u] / total[:, 4 * u : 4 * u + 1] for u in range(PER_OWNER)], axis=0
    ).astype(BF16)
    for s in range(SEQ):
        out_ref[s] = merged


def project_out(all_ref, weight_ref, out_ref, attended):
    attended[...] = all_ref[pl.ds(0, BATCH * TILES * ROWS), :].astype(F32)
    total = None
    for h in range(ROWS):
        rows = jnp.concatenate(
            [attended[pl.ds(t * ROWS + h, BATCH, stride=TILES * ROWS), :] for t in range(TILES)],
            axis=0,
        ).astype(BF16)
        part = jnp.dot(
            rows, weight_ref[h * LANES : (h + 1) * LANES, :], preferred_element_type=F32
        )
        total = part if total is None else total + part
    out_ref[...] = total.astype(BF16)


def add_pair(mine_ref, other_ref, out_ref):
    rounded = (mine_ref[...].astype(F32) + other_ref[...].astype(F32)).astype(BF16)
    for x in range(CHIPS):
        out_ref[x] = rounded


def add_groups(parts_ref, verify_ref, draft_ref, *halves):
    summed = parts_ref[0].astype(F32)
    for h in range(1, CHIPS):
        summed += parts_ref[h].astype(F32)
    rounded = summed.astype(BF16)
    for j in range(VERIFY):
        verify_ref[j] = rounded[j * BATCH : (j + 1) * BATCH]
    for k, half in enumerate(halves):
        at = slice(k * LANES, (k + 1) * LANES)
        half[...] = summed[TOKENS:, at]
        for b in range(BATCH):
            draft_ref[b, :, at] = half[pl.ds(b, DRAFT, stride=BATCH), :].astype(BF16)


VMEM = pl.BlockSpec(memory_space=pltpu.VMEM)
HBM = pl.BlockSpec(memory_space=pltpu.HBM)


def resident(array):
    return pltpu.with_memory_space_constraint(array, pltpu.VMEM)


def in_place(array):
    return pltpu.with_memory_space_constraint(array, pltpu.HBM)


def exchange(messages, axis):
    return lax.all_to_all(messages, axis, 0, 0, tiled=True)


def per_device(
    hidden_states,
    w_query,
    w_key,
    w_value,
    w_out,
    key_cache,
    value_cache,
    context_lengths,
    keep_blocks,
):
    width = hidden_states.shape[2]
    context = key_cache.shape[1]
    columns = w_out.shape[1]
    rows = hidden_states.transpose(1, 0, 2).reshape(TOKENS, width)
    half = LANES // 2
    inverse = (500000.0 ** (-(np.arange(LANES) % half) * 2.0 / LANES)).astype(np.float32)
    array = pltpu.VMEM
    parts, cosine, sine, live, kept, fresh = pl.pallas_call(
        project,
        out_shape=(
            array((SEQ, MESSAGE, LANES), BF16),
            array((MESSAGE, LANES), F32),
            array((MESSAGE, LANES), F32),
            array((BATCH, context), F32),
            array((BATCH, context), F32),
            array((ROWS, LANES), F32),
        ),
        in_specs=[HBM] * 7,
        out_specs=(VMEM,) * 6,
        scratch_shapes=[
            pltpu.VMEM((TOKENS, width), BF16),
            pltpu.VMEM(w_query.shape, BF16),
            pltpu.VMEM(w_key.shape, BF16),
            pltpu.VMEM(w_value.shape, BF16),
            pltpu.SMEM(context_lengths.shape, jnp.int32),
            pltpu.SMEM(keep_blocks.shape, jnp.int32),
            pltpu.VMEM((1, LANES), F32),
            pltpu.VMEM((SEQ * MESSAGE, LANES), F32),
            pltpu.SemaphoreType.DMA((7,)),
        ],
        name="project",
        compiler_params=pltpu.CompilerParams(vmem_limit_bytes=8 << 20),
    )(
        *(
            in_place(operand)
            for operand in (
                rows, w_query, w_key, w_value, context_lengths, keep_blocks,
                jnp.asarray(inverse).reshape(1, LANES),
            )
        )
    )
    parts = exchange(parts, "seq")
    rotated = pl.pallas_call(
        rotate,
        out_shape=pltpu.VMEM((SEQ, MESSAGE, LANES), BF16),
        in_specs=[VMEM] * 3,
        out_specs=VMEM,
        name="rotate",
        cost_estimate=pl.CostEstimate(
            flops=1000000000, transcendentals=0, bytes_accessed=64000000
        ),
        compiler_params=pltpu.CompilerParams(vmem_limit_bytes=8 << 20),
    )(resident(parts), resident(cosine), resident(sine))
    rotated = exchange(rotated, "seq")
    partial = pl.pallas_call(
        attend,
        out_shape=pltpu.VMEM((SEQ, (PER_OWNER + 1) * ROWS, LANES), BF16),
        in_specs=[VMEM] * 6,
        out_specs=VMEM,
        scratch_shapes=[
            pltpu.VMEM((BATCH, VERIFY * ROWS, context), F32),
            pltpu.VMEM((BATCH, TILES * ROWS, context), BF16),
        ],
        name="attend",
        compiler_params=pltpu.CompilerParams(vmem_limit_bytes=16 << 20),
    )(
        resident(live),
        resident(kept),
        resident(fresh),
        resident(rotated.reshape(SEQ * MESSAGE, LANES)),
        resident(key_cache),
        resident(value_cache),
    )
    partial = exchange(partial, "seq")
    merged = pl.pallas_call(
        merge,
        out_shape=pltpu.VMEM((SEQ, PER_OWNER * ROWS, LANES), BF16),
        in_specs=[VMEM],
        out_specs=VMEM,
        name="merge",
        compiler_params=pltpu.CompilerParams(vmem_limit_bytes=8 << 20),
    )(resident(partial))
    merged = exchange(merged, "seq").reshape(SEQ * PER_OWNER * ROWS, LANES)
    groups = pl.pallas_call(
        project_out,
        out_shape=pltpu.VMEM((BATCH * TILES, columns), BF16),
        in_specs=[VMEM, VMEM],
        out_specs=VMEM,
        scratch_shapes=[pltpu.VMEM((BATCH * TILES * ROWS, LANES), F32)],
        name="project_out",
        compiler_params=pltpu.CompilerParams(vmem_limit_bytes=8 << 20),
    )(resident(merged), resident(w_out))
    other = lax.ppermute(groups, "head", [(h, h ^ 1) for h in range(HEADS)])
    pairs = pl.pallas_call(
        add_pair,
        out_shape=pltpu.VMEM((CHIPS, BATCH * TILES, columns), BF16),
        in_specs=[VMEM, VMEM],
        out_specs=VMEM,
        name="add_pair",
        compiler_params=pltpu.CompilerParams(vmem_limit_bytes=8 << 20),
    )(resident(groups), resident(other))
    across = [[x * CORES + c for x in range(CHIPS)] for c in range(CORES)]
    pairs = lax.all_to_all(pairs, "head", 0, 0, tiled=True, axis_index_groups=across)
    verify_out, draft_out = pl.pallas_call(
        add_groups,
        out_shape=(
            jax.ShapeDtypeStruct((VERIFY, BATCH, columns), BF16),
            jax.ShapeDtypeStruct((BATCH, DRAFT, columns), BF16),
        ),
        in_specs=[VMEM],
        out_specs=(VMEM, VMEM),
        scratch_shapes=[pltpu.VMEM((DRAFT * BATCH, LANES), F32)] * (columns // LANES),
        name="add_groups",
        compiler_params=pltpu.CompilerParams(vmem_limit_bytes=8 << 20),
    )(resident(pairs))
    return verify_out.transpose(1, 0, 2), draft_out


def solution(mesh):
    placed = (
        P(None, None, "seq"),
        P("seq", "head"),
        P("seq", "head"),
        P("seq", "head"),
        P("head", "seq"),
        P(None, "seq", "head"),
        P(None, "seq", "head"),
        P(),
        P(None, "seq"),
    )
    return jax.shard_map(
        per_device,
        mesh=mesh,
        in_specs=placed,
        out_specs=(P(None, None, "seq"), P(None, None, "seq")),
        check_vma=False,
    )
```

```python
import jax
import jax.numpy as jnp
import numpy as np
from jax import lax
from jax.experimental import pallas as pl
from jax.experimental.pallas import tpu as pltpu
from jax.sharding import PartitionSpec as P

LANES = 128
ROWS = 8
BATCH = 8
VERIFY = 5
DRAFT = 4
TILES = VERIFY + DRAFT
SEQ = 32
HEADS = 8
CORES = 2
CHIPS = HEADS // CORES
TOKENS = BATCH * VERIFY
QUERY_ROWS = TOKENS * ROWS
OWNERS = SEQ // BATCH
PAIRS = TILES * ROWS // OWNERS
SUB = 4
STRIPS = 5
SLOTS = 24
MESSAGE = 16
NEGATIVE = -(2.0**100)
SCALE = LANES**-0.5
LOG2E = float(np.log2(np.e))
F32 = jnp.float32
BF16 = jnp.bfloat16


def project(
    hidden_hbm, query_hbm, key_hbm, value_hbm, lengths_hbm, keep_hbm, inverse_hbm,
    out_ref, cosine_ref, sine_ref, live_ref, kept_ref, fresh_ref,
    hidden_ref, query_ref, key_ref, value_ref, lengths_ref, keep_ref, inverse_ref, flat, sems,
):
    pairs = (
        (lengths_hbm, lengths_ref),
        (keep_hbm, keep_ref),
        (inverse_hbm, inverse_ref),
        (hidden_hbm, hidden_ref),
        (query_hbm, query_ref),
        (key_hbm, key_ref),
        (value_hbm, value_ref),
    )
    loads = [
        pltpu.make_async_copy(source, target, sems.at[i])
        for i, (source, target) in enumerate(pairs)
    ]
    for load in loads:
        load.start()
    for load in loads[:3]:
        load.wait()
    here = lax.axis_index("seq")
    row = lax.broadcasted_iota(jnp.int32, (ROWS, LANES), 0)
    lane = lax.broadcasted_iota(jnp.int32, (ROWS, LANES), 1)
    lengths = jnp.zeros((ROWS, LANES), jnp.int32)
    for b in range(BATCH):
        lengths = jnp.where(row == b, lengths_ref[b], lengths)
    for half in range(MESSAGE // ROWS):
        tile = here * (MESSAGE // ROWS) + half
        is_query = tile < TOKENS
        token = jnp.where(is_query, tile, 0)
        query_position = lengths_ref[lax.rem(token, BATCH)] + token // BATCH
        position = jnp.where(is_query, query_position, lengths + (tile - TOKENS))
        angle = position.astype(F32) * inverse_ref[...]
        plain = tile >= TOKENS + VERIFY
        at = slice(half * ROWS, (half + 1) * ROWS)
        sine = jnp.sin(angle)
        cosine_ref[at, :] = jnp.where(plain, 1.0, jnp.cos(angle))
        sine_ref[at, :] = jnp.where(plain, 0.0, jnp.where(lane < LANES // 2, -sine, sine))
    blocks = live_ref.shape[1] // LANES
    for c in range(blocks):
        at = slice(c * LANES, (c + 1) * LANES)
        live = jnp.where((here * blocks + c) * LANES + lane < lengths, 0.0, NEGATIVE)
        live_ref[:, at] = live
        keep = jnp.zeros((ROWS, LANES), jnp.int32)
        for b in range(BATCH):
            keep = jnp.where(row == b, keep_ref[b, c], keep)
        kept_ref[:, at] = jnp.where(keep > 0, 0.0, NEGATIVE)
    fresh_ref[...] = jnp.full((ROWS, LANES), jnp.where(here == 0, 0.0, NEGATIVE))
    for load in loads[3:]:
        load.wait()
    rows = hidden_ref[...]
    query = jnp.dot(rows, query_ref[...], preferred_element_type=F32)
    for h in range(ROWS):
        flat[pl.ds(h, TOKENS, stride=ROWS), :] = query[:, h * LANES : (h + 1) * LANES]
    flat[pl.ds(QUERY_ROWS, TOKENS), :] = jnp.dot(rows, key_ref[...], preferred_element_type=F32)
    flat[pl.ds(QUERY_ROWS + TOKENS, TOKENS), :] = jnp.dot(
        rows, value_ref[...], preferred_element_type=F32
    )
    used = QUERY_ROWS + 2 * TOKENS
    flat[pl.ds(used, SEQ * MESSAGE - used), :] = jnp.zeros((SEQ * MESSAGE - used, LANES), F32)
    out_ref[...] = flat[...].reshape(SEQ, MESSAGE, LANES).astype(out_ref.dtype)


def rotate(parts_ref, cosine_ref, sine_ref, out_ref):
    total = parts_ref[0].astype(F32)
    for s in range(1, SEQ):
        total += parts_ref[s].astype(F32)
    swapped = pltpu.roll(total, LANES // 2, 1)
    rotated = (total * cosine_ref[...] + swapped * sine_ref[...]).astype(BF16)
    for s in range(SEQ):
        out_ref[s] = rotated


def split(value):
    high = value.astype(BF16).astype(F32)
    return high, (value - high).astype(BF16).astype(F32)


def attend(
    live_ref, kept_ref, fresh_ref, all_ref, keys, values,
    out_ref, scores, weights, results, tails,
):
    blocks = keys.shape[1] // LANES
    lane = lax.broadcasted_iota(jnp.int32, (ROWS, LANES), 1)
    lane_row = lax.rem(lane, BATCH)
    padding = jnp.zeros((LANES - TOKENS, LANES), BF16)
    new_keys = jnp.concatenate([all_ref[pl.ds(QUERY_ROWS, TOKENS), :], padding], axis=0)
    new_values = jnp.concatenate([all_ref[pl.ds(QUERY_ROWS + TOKENS, TOKENS), :], padding], axis=0)
    transposed = (((1,), (1,)), ((), ()))
    exponent = SCALE * LOG2E

    def tile(j, b):
        return pl.ds((j * BATCH + b) * ROWS, ROWS)

    new_scores = (
        lax.dot_general(
            all_ref[pl.ds(0, QUERY_ROWS), :], new_keys, transposed, preferred_element_type=F32
        )
        * exponent
    )
    for b in range(BATCH):
        query = jnp.concatenate([all_ref[tile(j, b), :] for j in range(VERIFY)], axis=0)
        scores[b] = (
            lax.dot_general(query, keys[b], transposed, preferred_element_type=F32) * exponent
            + live_ref[b : b + 1, :]
        )
    kept, fresh, bases = [], [], []
    for b in range(BATCH):
        kept.append([kept_ref[b : b + 1, c * LANES : (c + 1) * LANES] for c in range(blocks)])
        rows = []
        for j in range(VERIFY):
            at = (j * BATCH + b) * ROWS
            seen = (lane_row == b) & (lane < (j + 1) * BATCH)
            rows.append(jnp.where(seen, new_scores[at : at + ROWS] + fresh_ref[...], NEGATIVE))
        rows = jnp.concatenate(rows, axis=0)
        target, draft = rows, rows[: DRAFT * ROWS]
        fresh.append(jnp.concatenate([target, draft], axis=0))
        for c in range(blocks):
            block = scores[b, :, c * LANES : (c + 1) * LANES]
            target = jnp.maximum(target, block)
            draft = jnp.maximum(draft, block[: DRAFT * ROWS] + kept[b][c])
        peak = jnp.max(jnp.concatenate([target, draft], axis=0), axis=1, keepdims=True)
        bases.append(split(peak))
    totals, fresh_weights = [], []
    for b in range(BATCH):
        base = bases[b][0] + bases[b][1]
        base_target = base[: VERIFY * ROWS]
        base_draft = base[VERIFY * ROWS :]
        new_weights = jnp.exp2(fresh[b] - base)
        fresh_weights.append(new_weights)
        sums = new_weights
        for c in range(blocks):
            at = slice(c * LANES, (c + 1) * LANES)
            block = scores[b, :, at]
            result = jnp.concatenate(
                [
                    jnp.exp2(block - base_target),
                    jnp.exp2(block[: DRAFT * ROWS] + kept[b][c] - base_draft),
                ],
                axis=0,
            )
            sums += result
            weights[b, :, at] = result.astype(BF16)
        totals.append(jnp.sum(sums, axis=1, keepdims=True))
    fresh_result = jnp.dot(
        jnp.concatenate(fresh_weights, axis=0).astype(BF16),
        new_values,
        preferred_element_type=F32,
    )
    rows = TILES * ROWS
    packed = jnp.zeros((rows, LANES), F32)
    lanes = lax.broadcasted_iota(jnp.int32, (rows, LANES), 1)
    for b in range(BATCH):
        results[pl.ds(b * rows, rows), :] = (
            jnp.dot(weights[b], values[b], preferred_element_type=F32)
            + fresh_result[b * rows : (b + 1) * rows]
        )
        for k, value in enumerate(bases[b] + split(totals[b])):
            packed = jnp.where(lanes == k * BATCH + b, value, packed)
    stats = jnp.concatenate([packed, jnp.zeros((LANES - rows, LANES), F32)], axis=0).T
    for i in range(OWNERS):
        near = stats[: 4 * BATCH]
        if i:
            near = pltpu.roll(near, LANES - i * PAIRS, 1)
        far = pltpu.roll(near, LANES // 2, 1)
        for r in range(2):
            high = near[2 * r * BATCH : (2 * r + 1) * BATCH]
            low = far[(2 * r + 1) * BATCH : (2 * r + 2) * BATCH]
            every = pl.ds(i * SUB + 2 + r, BATCH, stride=OWNERS * SUB)
            tails[every, :] = jnp.where(lane < LANES // 2, high, low)
            tails[pl.ds(i * SUB + r, BATCH, stride=OWNERS * SUB), :] = results[
                pl.ds(i * PAIRS + 16 + r, BATCH, stride=rows), :
            ]
    for d in range(SEQ):
        for k in range(STRIPS):
            if k < STRIPS - 1:
                strip = results[pl.ds(d * PAIRS + k * SUB, SUB), :]
            else:
                strip = tails[pl.ds(d * SUB, SUB), :]
            out_ref[d, :, k * LANES : (k + 1) * LANES] = strip.astype(BF16)


def merge(parts_ref, out_ref, parts):
    for s in range(SEQ):
        for k in range(STRIPS):
            strip = parts_ref[s, :, k * LANES : (k + 1) * LANES]
            parts[pl.ds(s * SLOTS + k * SUB, SUB), :] = strip.astype(F32)
        parts[pl.ds(s * SLOTS + STRIPS * SUB, SUB), :] = jnp.zeros((SUB, LANES), F32)
    peaks = parts[pl.ds(PAIRS, SEQ, stride=SLOTS), :]
    peaks += pltpu.roll(peaks, LANES // 2, 1)
    totals = parts[pl.ds(PAIRS + 1, SEQ, stride=SLOTS), :]
    totals += pltpu.roll(totals, LANES // 2, 1)
    factors = jnp.exp2(peaks - jnp.max(peaks, axis=0, keepdims=True))
    total = jnp.sum(factors * totals, axis=0, keepdims=True)
    factors = factors / jnp.where(total > 0.0, total, 1.0)
    factors = jnp.concatenate([factors, jnp.zeros((LANES - SEQ, LANES), F32)], axis=0).T
    factors = factors[:SLOTS]
    merged = jnp.zeros((SLOTS, LANES), F32)
    for s in range(SEQ):
        merged += parts[pl.ds(s * SLOTS, SLOTS), :] * factors[:, s : s + 1]
    merged = merged.astype(BF16)
    for k in range(STRIPS):
        strip = merged[k * SUB : (k + 1) * SUB]
        for s in range(SEQ):
            out_ref[s, :, k * LANES : (k + 1) * LANES] = strip


def project_out(all_ref, weight_ref, out_ref, attended):
    for d in range(SEQ):
        for k in range(STRIPS):
            size = min(SUB, PAIRS - k * SUB)
            strip = all_ref[d, :, k * LANES : (k + 1) * LANES].astype(F32)
            attended[pl.ds(d * PAIRS + k * SUB, size), :] = strip[:size]
    total = None
    for h in range(ROWS):
        rows = jnp.concatenate(
            [attended[pl.ds(t * ROWS + h, BATCH, stride=TILES * ROWS), :] for t in range(TILES)],
            axis=0,
        ).astype(BF16)
        part = jnp.dot(
            rows, weight_ref[h * LANES : (h + 1) * LANES, :], preferred_element_type=F32
        )
        total = part if total is None else total + part
    out_ref[...] = total.astype(BF16)


def add_pair(mine_ref, other_ref, out_ref):
    rounded = (mine_ref[...].astype(F32) + other_ref[...].astype(F32)).astype(BF16)
    for x in range(CHIPS):
        out_ref[x] = rounded


def add_groups(parts_ref, verify_ref, draft_ref, *halves):
    summed = parts_ref[0].astype(F32)
    for h in range(1, CHIPS):
        summed += parts_ref[h].astype(F32)
    rounded = summed.astype(BF16)
    for j in range(VERIFY):
        verify_ref[j] = rounded[j * BATCH : (j + 1) * BATCH]
    for k, half in enumerate(halves):
        at = slice(k * LANES, (k + 1) * LANES)
        half[...] = summed[TOKENS:, at]
        for b in range(BATCH):
            draft_ref[b, :, at] = half[pl.ds(b, DRAFT, stride=BATCH), :].astype(BF16)


VMEM = pl.BlockSpec(memory_space=pltpu.VMEM)
HBM = pl.BlockSpec(memory_space=pltpu.HBM)


def resident(array):
    return pltpu.with_memory_space_constraint(array, pltpu.VMEM)


def in_place(array):
    return pltpu.with_memory_space_constraint(array, pltpu.HBM)


def exchange(messages, axis):
    return lax.all_to_all(messages, axis, 0, 0, tiled=True)


def per_device(
    hidden_states,
    w_query,
    w_key,
    w_value,
    w_out,
    key_cache,
    value_cache,
    context_lengths,
    keep_blocks,
):
    width = hidden_states.shape[2]
    context = key_cache.shape[1]
    columns = w_out.shape[1]
    rows = hidden_states.transpose(1, 0, 2).reshape(TOKENS, width)
    half = LANES // 2
    inverse = (500000.0 ** (-(np.arange(LANES) % half) * 2.0 / LANES)).astype(np.float32)
    array = pltpu.VMEM
    parts, cosine, sine, live, kept, fresh = pl.pallas_call(
        project,
        out_shape=(
            array((SEQ, MESSAGE, LANES), BF16),
            array((MESSAGE, LANES), F32),
            array((MESSAGE, LANES), F32),
            array((BATCH, context), F32),
            array((BATCH, context), F32),
            array((ROWS, LANES), F32),
        ),
        in_specs=[HBM] * 7,
        out_specs=(VMEM,) * 6,
        scratch_shapes=[
            pltpu.VMEM((TOKENS, width), BF16),
            pltpu.VMEM(w_query.shape, BF16),
            pltpu.VMEM(w_key.shape, BF16),
            pltpu.VMEM(w_value.shape, BF16),
            pltpu.SMEM(context_lengths.shape, jnp.int32),
            pltpu.SMEM(keep_blocks.shape, jnp.int32),
            pltpu.VMEM((1, LANES), F32),
            pltpu.VMEM((SEQ * MESSAGE, LANES), F32),
            pltpu.SemaphoreType.DMA((7,)),
        ],
        name="project",
        compiler_params=pltpu.CompilerParams(vmem_limit_bytes=8 << 20),
    )(
        *(
            in_place(operand)
            for operand in (
                rows, w_query, w_key, w_value, context_lengths, keep_blocks,
                jnp.asarray(inverse).reshape(1, LANES),
            )
        )
    )
    parts = exchange(parts, "seq")
    rotated = pl.pallas_call(
        rotate,
        out_shape=pltpu.VMEM((SEQ, MESSAGE, LANES), BF16),
        in_specs=[VMEM] * 3,
        out_specs=VMEM,
        name="rotate",
        cost_estimate=pl.CostEstimate(
            flops=1000000000, transcendentals=0, bytes_accessed=64000000
        ),
        compiler_params=pltpu.CompilerParams(vmem_limit_bytes=8 << 20),
    )(resident(parts), resident(cosine), resident(sine))
    rotated = exchange(rotated, "seq")
    partial = pl.pallas_call(
        attend,
        out_shape=pltpu.VMEM((SEQ, SUB, STRIPS * LANES), BF16),
        in_specs=[VMEM] * 6,
        out_specs=VMEM,
        scratch_shapes=[
            pltpu.VMEM((BATCH, VERIFY * ROWS, context), F32),
            pltpu.VMEM((BATCH, TILES * ROWS, context), BF16),
            pltpu.VMEM((BATCH * TILES * ROWS, LANES), F32),
            pltpu.VMEM((SEQ * SUB, LANES), F32),
        ],
        name="attend",
        compiler_params=pltpu.CompilerParams(vmem_limit_bytes=16 << 20),
    )(
        resident(live),
        resident(kept),
        resident(fresh),
        resident(rotated.reshape(SEQ * MESSAGE, LANES)),
        resident(key_cache),
        resident(value_cache),
    )
    partial = exchange(partial, "seq")
    merged = pl.pallas_call(
        merge,
        out_shape=pltpu.VMEM((SEQ, SUB, STRIPS * LANES), BF16),
        in_specs=[VMEM],
        out_specs=VMEM,
        scratch_shapes=[pltpu.VMEM((SEQ * SLOTS, LANES), F32)],
        name="merge",
        compiler_params=pltpu.CompilerParams(vmem_limit_bytes=8 << 20),
    )(resident(partial))
    merged = exchange(merged, "seq")
    groups = pl.pallas_call(
        project_out,
        out_shape=pltpu.VMEM((BATCH * TILES, columns), BF16),
        in_specs=[VMEM, VMEM],
        out_specs=VMEM,
        scratch_shapes=[pltpu.VMEM((BATCH * TILES * ROWS, LANES), F32)],
        name="project_out",
        compiler_params=pltpu.CompilerParams(vmem_limit_bytes=8 << 20),
    )(resident(merged), resident(w_out))
    other = lax.ppermute(groups, "head", [(h, h ^ 1) for h in range(HEADS)])
    pairs = pl.pallas_call(
        add_pair,
        out_shape=pltpu.VMEM((CHIPS, BATCH * TILES, columns), BF16),
        in_specs=[VMEM, VMEM],
        out_specs=VMEM,
        name="add_pair",
        compiler_params=pltpu.CompilerParams(vmem_limit_bytes=8 << 20),
    )(resident(groups), resident(other))
    across = [[x * CORES + c for x in range(CHIPS)] for c in range(CORES)]
    pairs = lax.all_to_all(pairs, "head", 0, 0, tiled=True, axis_index_groups=across)
    verify_out, draft_out = pl.pallas_call(
        add_groups,
        out_shape=(
            jax.ShapeDtypeStruct((VERIFY, BATCH, columns), BF16),
            jax.ShapeDtypeStruct((BATCH, DRAFT, columns), BF16),
        ),
        in_specs=[VMEM],
        out_specs=(VMEM, VMEM),
        scratch_shapes=[pltpu.VMEM((DRAFT * BATCH, LANES), F32)] * (columns // LANES),
        name="add_groups",
        compiler_params=pltpu.CompilerParams(vmem_limit_bytes=8 << 20),
    )(resident(pairs))
    return verify_out.transpose(1, 0, 2), draft_out


def solution(mesh):
    placed = (
        P(None, None, "seq"),
        P("seq", "head"),
        P("seq", "head"),
        P("seq", "head"),
        P("head", "seq"),
        P(None, "seq", "head"),
        P(None, "seq", "head"),
        P(),
        P(None, "seq"),
    )
    return jax.shard_map(
        per_device,
        mesh=mesh,
        in_specs=placed,
        out_specs=(P(None, None, "seq"), P(None, None, "seq")),
        check_vma=False,
    )
```

```python
import jax
import jax.numpy as jnp
import numpy as np
from jax import lax
from jax.experimental import pallas as pl
from jax.experimental.pallas import tpu as pltpu
from jax.sharding import PartitionSpec as P

LANES = 128
ROWS = 8
BATCH = 8
VERIFY = 5
DRAFT = 4
TILES = VERIFY + DRAFT
SEQ = 32
HEADS = 8
CORES = 2
CHIPS = HEADS // CORES
TOKENS = BATCH * VERIFY
QUERY_ROWS = TOKENS * ROWS
OWNERS = SEQ // BATCH
PAIRS = TILES * ROWS // OWNERS
SUB = 4
STRIPS = 5
SPARE = 72
SLOTS = 24
MESSAGE = 16
NEGATIVE = -(2.0**100)
SCALE = LANES**-0.5
LOG2E = float(np.log2(np.e))
F32 = jnp.float32
BF16 = jnp.bfloat16


def project(
    hidden_hbm, query_hbm, key_hbm, value_hbm, lengths_hbm, keep_hbm, inverse_hbm,
    out_ref, cosine_ref, sine_ref, live_ref, kept_ref, fresh_ref,
    hidden_ref, query_ref, key_ref, value_ref, lengths_ref, keep_ref, inverse_ref, flat, sems,
):
    pairs = (
        (lengths_hbm, lengths_ref),
        (keep_hbm, keep_ref),
        (inverse_hbm, inverse_ref),
        (hidden_hbm, hidden_ref),
        (query_hbm, query_ref),
        (key_hbm, key_ref),
        (value_hbm, value_ref),
    )
    loads = [
        pltpu.make_async_copy(source, target, sems.at[i])
        for i, (source, target) in enumerate(pairs)
    ]
    for load in loads:
        load.start()
    for load in loads[:3]:
        load.wait()
    here = lax.axis_index("seq")
    row = lax.broadcasted_iota(jnp.int32, (ROWS, LANES), 0)
    lane = lax.broadcasted_iota(jnp.int32, (ROWS, LANES), 1)
    lengths = jnp.zeros((ROWS, LANES), jnp.int32)
    for b in range(BATCH):
        lengths = jnp.where(row == b, lengths_ref[b], lengths)
    for half in range(MESSAGE // ROWS):
        tile = here * (MESSAGE // ROWS) + half
        is_query = tile < TOKENS
        token = jnp.where(is_query, tile, 0)
        query_position = lengths_ref[lax.rem(token, BATCH)] + token // BATCH
        position = jnp.where(is_query, query_position, lengths + (tile - TOKENS))
        angle = position.astype(F32) * inverse_ref[...]
        plain = tile >= TOKENS + VERIFY
        at = slice(half * ROWS, (half + 1) * ROWS)
        sine = jnp.sin(angle)
        cosine_ref[at, :] = jnp.where(plain, 1.0, jnp.cos(angle))
        sine_ref[at, :] = jnp.where(plain, 0.0, jnp.where(lane < LANES // 2, -sine, sine))
    blocks = live_ref.shape[1] // LANES
    for c in range(blocks):
        at = slice(c * LANES, (c + 1) * LANES)
        live = jnp.where((here * blocks + c) * LANES + lane < lengths, 0.0, NEGATIVE)
        live_ref[:, at] = live
        keep = jnp.zeros((ROWS, LANES), jnp.int32)
        for b in range(BATCH):
            keep = jnp.where(row == b, keep_ref[b, c], keep)
        kept_ref[:, at] = jnp.where(keep > 0, 0.0, NEGATIVE)
    fresh_ref[...] = jnp.full((ROWS, LANES), jnp.where(here == 0, 0.0, NEGATIVE))
    for load in loads[3:]:
        load.wait()
    rows = hidden_ref[...]
    query = jnp.dot(rows, query_ref[...], preferred_element_type=F32)
    for h in range(ROWS):
        flat[pl.ds(h, TOKENS, stride=ROWS), :] = query[:, h * LANES : (h + 1) * LANES]
    flat[pl.ds(QUERY_ROWS, TOKENS), :] = jnp.dot(rows, key_ref[...], preferred_element_type=F32)
    flat[pl.ds(QUERY_ROWS + TOKENS, TOKENS), :] = jnp.dot(
        rows, value_ref[...], preferred_element_type=F32
    )
    used = QUERY_ROWS + 2 * TOKENS
    flat[pl.ds(used, SEQ * MESSAGE - used), :] = jnp.zeros((SEQ * MESSAGE - used, LANES), F32)
    out_ref[...] = flat[...].reshape(SEQ, MESSAGE, LANES).astype(out_ref.dtype)


def rotate(parts_ref, cosine_ref, sine_ref, out_ref):
    total = parts_ref[0].astype(F32)
    for s in range(1, SEQ):
        total += parts_ref[s].astype(F32)
    swapped = pltpu.roll(total, LANES // 2, 1)
    rotated = (total * cosine_ref[...] + swapped * sine_ref[...]).astype(BF16)
    for s in range(SEQ):
        out_ref[s] = rotated


def split(value):
    high = value.astype(BF16).astype(F32)
    return high, (value - high).astype(BF16).astype(F32)


def attend(
    live_ref, kept_ref, fresh_ref, all_ref, keys, values,
    out_ref, scores, weights, results, tails,
):
    blocks = keys.shape[1] // LANES
    lane = lax.broadcasted_iota(jnp.int32, (ROWS, LANES), 1)
    lane_row = lax.rem(lane, BATCH)
    padding = jnp.zeros((LANES - TOKENS, LANES), BF16)
    new_keys = jnp.concatenate([all_ref[pl.ds(QUERY_ROWS, TOKENS), :], padding], axis=0)
    new_values = jnp.concatenate([all_ref[pl.ds(QUERY_ROWS + TOKENS, TOKENS), :], padding], axis=0)
    transposed = (((1,), (1,)), ((), ()))
    exponent = SCALE * LOG2E

    def tile(j, b):
        return pl.ds((j * BATCH + b) * ROWS, ROWS)

    new_scores = (
        lax.dot_general(
            all_ref[pl.ds(0, QUERY_ROWS), :], new_keys, transposed, preferred_element_type=F32
        )
        * exponent
    )
    for b in range(BATCH):
        query = jnp.concatenate([all_ref[tile(j, b), :] for j in range(VERIFY)], axis=0)
        scores[b] = (
            lax.dot_general(query, keys[b], transposed, preferred_element_type=F32) * exponent
            + live_ref[b : b + 1, :]
        )
    kept, fresh, bases = [], [], []
    for b in range(BATCH):
        kept.append([kept_ref[b : b + 1, c * LANES : (c + 1) * LANES] for c in range(blocks)])
        rows = []
        for j in range(VERIFY):
            at = (j * BATCH + b) * ROWS
            seen = (lane_row == b) & (lane < (j + 1) * BATCH)
            rows.append(jnp.where(seen, new_scores[at : at + ROWS] + fresh_ref[...], NEGATIVE))
        rows = jnp.concatenate(rows, axis=0)
        target, draft = rows, rows[: DRAFT * ROWS]
        fresh.append(jnp.concatenate([target, draft], axis=0))
        for c in range(blocks):
            block = scores[b, :, c * LANES : (c + 1) * LANES]
            target = jnp.maximum(target, block)
            draft = jnp.maximum(draft, block[: DRAFT * ROWS] + kept[b][c])
        peak = jnp.max(jnp.concatenate([target, draft], axis=0), axis=1, keepdims=True)
        bases.append(split(peak))
    totals, fresh_weights = [], []
    for b in range(BATCH):
        base = bases[b][0] + bases[b][1]
        base_target = base[: VERIFY * ROWS]
        base_draft = base[VERIFY * ROWS :]
        new_weights = jnp.exp2(fresh[b] - base)
        fresh_weights.append(new_weights)
        sums = new_weights
        for c in range(blocks):
            at = slice(c * LANES, (c + 1) * LANES)
            block = scores[b, :, at]
            result = jnp.concatenate(
                [
                    jnp.exp2(block - base_target),
                    jnp.exp2(block[: DRAFT * ROWS] + kept[b][c] - base_draft),
                ],
                axis=0,
            )
            sums += result
            weights[b, :, at] = result.astype(BF16)
        totals.append(jnp.sum(sums, axis=1, keepdims=True))
    fresh_result = jnp.dot(
        jnp.concatenate(fresh_weights, axis=0).astype(BF16),
        new_values,
        preferred_element_type=F32,
    )
    rows = TILES * ROWS
    packed = jnp.zeros((rows, LANES), F32)
    lanes = lax.broadcasted_iota(jnp.int32, (rows, LANES), 1)
    for b in range(BATCH):
        results[pl.ds(b * rows, rows), :] = (
            jnp.dot(weights[b], values[b], preferred_element_type=F32)
            + fresh_result[b * rows : (b + 1) * rows]
        )
        for k, value in enumerate(bases[b] + split(totals[b])):
            packed = jnp.where(lanes == k * BATCH + b, value, packed)
    stats = jnp.concatenate([packed, jnp.zeros((LANES - rows, LANES), F32)], axis=0).T
    for i in range(OWNERS):
        near = stats[: 4 * BATCH]
        if i:
            near = pltpu.roll(near, LANES - i * PAIRS, 1)
        far = pltpu.roll(near, LANES // 2, 1)
        for r in range(2):
            high = near[2 * r * BATCH : (2 * r + 1) * BATCH]
            low = far[(2 * r + 1) * BATCH : (2 * r + 2) * BATCH]
            every = pl.ds(i * SUB + 2 + r, BATCH, stride=OWNERS * SUB)
            tails[every, :] = jnp.where(lane < LANES // 2, high, low)
            tails[pl.ds(i * SUB + r, BATCH, stride=OWNERS * SUB), :] = results[
                pl.ds(i * PAIRS + 16 + r, BATCH, stride=rows), :
            ]
    for d in range(SEQ):
        for k in range(STRIPS):
            if k < STRIPS - 1:
                strip = results[pl.ds(d * PAIRS + k * SUB, SUB), :]
            else:
                strip = tails[pl.ds(d * SUB, SUB), :]
            out_ref[d, :, k * LANES : (k + 1) * LANES] = strip.astype(BF16)


def merge(parts_ref, out_ref, parts):
    for s in range(SEQ):
        for k in range(STRIPS):
            strip = parts_ref[s, :, k * LANES : (k + 1) * LANES]
            parts[pl.ds(s * SLOTS + k * SUB, SUB), :] = strip.astype(F32)
        parts[pl.ds(s * SLOTS + STRIPS * SUB, SUB), :] = jnp.zeros((SUB, LANES), F32)
    peaks = parts[pl.ds(PAIRS, SEQ, stride=SLOTS), :]
    peaks += pltpu.roll(peaks, LANES // 2, 1)
    totals = parts[pl.ds(PAIRS + 1, SEQ, stride=SLOTS), :]
    totals += pltpu.roll(totals, LANES // 2, 1)
    factors = jnp.exp2(peaks - jnp.max(peaks, axis=0, keepdims=True))
    total = jnp.sum(factors * totals, axis=0, keepdims=True)
    factors = factors / jnp.where(total > 0.0, total, 1.0)
    factors = jnp.concatenate([factors, jnp.zeros((LANES - SEQ, LANES), F32)], axis=0).T
    factors = factors[:SLOTS]
    merged = jnp.zeros((SLOTS, LANES), F32)
    for s in range(SEQ):
        merged += parts[pl.ds(s * SLOTS, SLOTS), :] * factors[:, s : s + 1]
    merged = merged.astype(BF16)
    for k in range(STRIPS):
        strip = merged[k * SUB : (k + 1) * SUB]
        for s in range(SEQ):
            out_ref[s, :, k * LANES : (k + 1) * LANES] = strip


def project_out(all_ref, weight_ref, out_ref, attended):
    for d in range(SEQ):
        for k in range(STRIPS):
            size = min(SUB, PAIRS - k * SUB)
            strip = all_ref[d, :, k * LANES : (k + 1) * LANES].astype(F32)
            attended[pl.ds(d * PAIRS + k * SUB, size), :] = strip[:size]
    total = None
    for h in range(ROWS):
        rows = jnp.concatenate(
            [attended[pl.ds(t * ROWS + h, BATCH, stride=TILES * ROWS), :] for t in range(TILES)],
            axis=0,
        ).astype(BF16)
        part = jnp.dot(
            rows, weight_ref[h * LANES : (h + 1) * LANES, :], preferred_element_type=F32
        )
        total = part if total is None else total + part
    out_ref[...] = total.astype(BF16)


def add_pair(mine_ref, other_ref, out_ref):
    rounded = (mine_ref[...].astype(F32) + other_ref[...].astype(F32)).astype(BF16)
    for x in range(CHIPS):
        out_ref[x] = rounded


def add_groups(parts_ref, verify_ref, draft_ref, *halves):
    summed = parts_ref[0].astype(F32)
    for h in range(1, CHIPS):
        summed += parts_ref[h].astype(F32)
    rounded = summed.astype(BF16)
    for j in range(VERIFY):
        verify_ref[j] = rounded[j * BATCH : (j + 1) * BATCH]
    for k, half in enumerate(halves):
        at = slice(k * LANES, (k + 1) * LANES)
        half[pl.ds(0, DRAFT * BATCH), :] = summed[TOKENS:, at]
        for b in range(BATCH):
            draft_ref[b, :, at] = half[pl.ds(b, DRAFT, stride=BATCH), :].astype(BF16)


VMEM = pl.BlockSpec(memory_space=pltpu.VMEM)
HBM = pl.BlockSpec(memory_space=pltpu.HBM)


def resident(array):
    return pltpu.with_memory_space_constraint(array, pltpu.VMEM)


def in_place(array):
    return pltpu.with_memory_space_constraint(array, pltpu.HBM)


def exchange(messages, axis):
    return lax.all_to_all(messages, axis, 0, 0, tiled=True)


def per_device(
    hidden_states,
    w_query,
    w_key,
    w_value,
    w_out,
    key_cache,
    value_cache,
    context_lengths,
    keep_blocks,
):
    width = hidden_states.shape[2]
    context = key_cache.shape[1]
    columns = w_out.shape[1]
    rows = hidden_states.transpose(1, 0, 2).reshape(TOKENS, width)
    half = LANES // 2
    inverse = (500000.0 ** (-(np.arange(LANES) % half) * 2.0 / LANES)).astype(np.float32)
    array = pltpu.VMEM
    parts, cosine, sine, live, kept, fresh = pl.pallas_call(
        project,
        out_shape=(
            array((SEQ, MESSAGE, LANES), F32),
            array((MESSAGE, LANES), F32),
            array((MESSAGE, LANES), F32),
            array((BATCH, context), F32),
            array((BATCH, context), F32),
            array((ROWS, LANES), F32),
        ),
        in_specs=[HBM] * 7,
        out_specs=(VMEM,) * 6,
        scratch_shapes=[
            pltpu.VMEM((TOKENS, width), BF16),
            pltpu.VMEM(w_query.shape, BF16),
            pltpu.VMEM(w_key.shape, BF16),
            pltpu.VMEM(w_value.shape, BF16),
            pltpu.SMEM(context_lengths.shape, jnp.int32),
            pltpu.SMEM(keep_blocks.shape, jnp.int32),
            pltpu.VMEM((1, LANES), F32),
            pltpu.VMEM((SEQ * MESSAGE, LANES), F32),
            pltpu.SemaphoreType.DMA((7,)),
        ],
        name="project",
        compiler_params=pltpu.CompilerParams(vmem_limit_bytes=8 << 20),
    )(
        *(
            in_place(operand)
            for operand in (
                rows, w_query, w_key, w_value, context_lengths, keep_blocks,
                jnp.asarray(inverse).reshape(1, LANES),
            )
        )
    )
    parts = exchange(parts, "seq")
    rotated = pl.pallas_call(
        rotate,
        out_shape=pltpu.VMEM((SEQ, MESSAGE, LANES), BF16),
        in_specs=[VMEM] * 3,
        out_specs=VMEM,
        name="rotate",
        cost_estimate=pl.CostEstimate(
            flops=1000000000, transcendentals=0, bytes_accessed=64000000
        ),
        compiler_params=pltpu.CompilerParams(vmem_limit_bytes=8 << 20),
    )(resident(parts), resident(cosine), resident(sine))
    rotated = exchange(rotated, "seq")
    partial = pl.pallas_call(
        attend,
        out_shape=pltpu.VMEM((SEQ, SUB, STRIPS * LANES), BF16),
        in_specs=[VMEM] * 6,
        out_specs=VMEM,
        scratch_shapes=[
            pltpu.VMEM((BATCH, VERIFY * ROWS, context), F32),
            pltpu.VMEM((BATCH, TILES * ROWS, context), BF16),
            pltpu.VMEM((BATCH * TILES * ROWS + SPARE, LANES), F32),
            pltpu.VMEM((SEQ * SUB + SPARE, LANES), F32),
        ],
        name="attend",
        compiler_params=pltpu.CompilerParams(vmem_limit_bytes=16 << 20),
    )(
        resident(live),
        resident(kept),
        resident(fresh),
        resident(rotated.reshape(SEQ * MESSAGE, LANES)),
        resident(key_cache),
        resident(value_cache),
    )
    partial = exchange(partial, "seq")
    merged = pl.pallas_call(
        merge,
        out_shape=pltpu.VMEM((SEQ, SUB, STRIPS * LANES), BF16),
        in_specs=[VMEM],
        out_specs=VMEM,
        scratch_shapes=[pltpu.VMEM((SEQ * SLOTS + SPARE, LANES), F32)],
        name="merge",
        compiler_params=pltpu.CompilerParams(vmem_limit_bytes=8 << 20),
    )(resident(partial))
    merged = exchange(merged, "seq")
    groups = pl.pallas_call(
        project_out,
        out_shape=pltpu.VMEM((BATCH * TILES, columns), BF16),
        in_specs=[VMEM, VMEM],
        out_specs=VMEM,
        scratch_shapes=[pltpu.VMEM((BATCH * TILES * ROWS + SPARE, LANES), F32)],
        name="project_out",
        compiler_params=pltpu.CompilerParams(vmem_limit_bytes=8 << 20),
    )(resident(merged), resident(w_out))
    other = lax.ppermute(groups, "head", [(h, h ^ 1) for h in range(HEADS)])
    pairs = pl.pallas_call(
        add_pair,
        out_shape=pltpu.VMEM((CHIPS, BATCH * TILES, columns), BF16),
        in_specs=[VMEM, VMEM],
        out_specs=VMEM,
        name="add_pair",
        compiler_params=pltpu.CompilerParams(vmem_limit_bytes=8 << 20),
    )(resident(groups), resident(other))
    across = [[x * CORES + c for x in range(CHIPS)] for c in range(CORES)]
    pairs = lax.all_to_all(pairs, "head", 0, 0, tiled=True, axis_index_groups=across)
    verify_out, draft_out = pl.pallas_call(
        add_groups,
        out_shape=(
            jax.ShapeDtypeStruct((VERIFY, BATCH, columns), BF16),
            jax.ShapeDtypeStruct((BATCH, DRAFT, columns), BF16),
        ),
        in_specs=[VMEM],
        out_specs=(VMEM, VMEM),
        scratch_shapes=[pltpu.VMEM((DRAFT * BATCH + SPARE, LANES), F32)] * (columns // LANES),
        name="add_groups",
        compiler_params=pltpu.CompilerParams(vmem_limit_bytes=8 << 20),
    )(resident(pairs))
    return verify_out.transpose(1, 0, 2), draft_out


def solution(mesh):
    placed = (
        P(None, None, "seq"),
        P("seq", "head"),
        P("seq", "head"),
        P("seq", "head"),
        P("head", "seq"),
        P(None, "seq", "head"),
        P(None, "seq", "head"),
        P(),
        P(None, "seq"),
    )
    return jax.shard_map(
        per_device,
        mesh=mesh,
        in_specs=placed,
        out_specs=(P(None, None, "seq"), P(None, None, "seq")),
        check_vma=False,
    )
```

```python
import jax
import jax.numpy as jnp
import numpy as np
from jax import lax
from jax.experimental import pallas as pl
from jax.experimental.pallas import tpu as pltpu
from jax.sharding import PartitionSpec as P

LANES = 128
ROWS = 8
BATCH = 8
VERIFY = 5
DRAFT = 4
TILES = VERIFY + DRAFT
SEQ = 32
HEADS = 8
CORES = 2
CHIPS = HEADS // CORES
TOKENS = BATCH * VERIFY
QUERY_ROWS = TOKENS * ROWS
OWNERS = SEQ // BATCH
PAIRS = TILES * ROWS // OWNERS
SUB = 4
STRIPS = 5
SPARE = 72
SLOTS = 24
QUERIES = QUERY_ROWS // SEQ
MESSAGE = 16
NEGATIVE = -(2.0**100)
SCALE = LANES**-0.5
LOG2E = float(np.log2(np.e))
F32 = jnp.float32
BF16 = jnp.bfloat16


def project(
    hidden_hbm, query_hbm, key_hbm, value_hbm, lengths_hbm, keep_hbm, inverse_hbm,
    out_ref, cosine_ref, sine_ref, live_ref, kept_ref, fresh_ref,
    hidden_ref, query_ref, key_ref, value_ref, lengths_ref, keep_ref, inverse_ref, flat, packed, sems,
):
    pairs = (
        (lengths_hbm, lengths_ref),
        (keep_hbm, keep_ref),
        (inverse_hbm, inverse_ref),
        (hidden_hbm, hidden_ref),
        (query_hbm, query_ref),
        (key_hbm, key_ref),
        (value_hbm, value_ref),
    )
    loads = [
        pltpu.make_async_copy(source, target, sems.at[i])
        for i, (source, target) in enumerate(pairs)
    ]
    for load in loads:
        load.start()
    for load in loads[:3]:
        load.wait()
    here = lax.axis_index("seq")
    row = lax.broadcasted_iota(jnp.int32, (ROWS, LANES), 0)
    lane = lax.broadcasted_iota(jnp.int32, (ROWS, LANES), 1)
    lengths = jnp.zeros((ROWS, LANES), jnp.int32)
    for b in range(BATCH):
        lengths = jnp.where(row == b, lengths_ref[b], lengths)
    mine, turn = here // OWNERS, lax.rem(here, OWNERS)
    slot = lax.broadcasted_iota(jnp.int32, (MESSAGE, LANES), 0)
    token = jnp.where(
        slot < QUERIES,
        jnp.right_shift(QUERIES * here + slot, 3),
        jnp.where(slot < QUERIES + 2, turn * BATCH + mine, DRAFT * BATCH + mine),
    )
    position = jnp.right_shift(token, 3)
    for b in range(BATCH):
        position += jnp.where(jnp.bitwise_and(token, 7) == b, lengths_ref[b], 0)
    angle = position.astype(F32) * inverse_ref[...]
    plain = (slot == QUERIES + 1) | (slot == QUERIES + 3)
    half = lax.broadcasted_iota(jnp.int32, (MESSAGE, LANES), 1) < LANES // 2
    sine = jnp.sin(angle)
    cosine_ref[...] = jnp.where(plain, 1.0, jnp.cos(angle))
    sine_ref[...] = jnp.where(plain, 0.0, jnp.where(half, -sine, sine))
    blocks = live_ref.shape[1] // LANES
    for c in range(blocks):
        at = slice(c * LANES, (c + 1) * LANES)
        live = jnp.where((here * blocks + c) * LANES + lane < lengths, 0.0, NEGATIVE)
        live_ref[:, at] = live
        keep = jnp.zeros((ROWS, LANES), jnp.int32)
        for b in range(BATCH):
            keep = jnp.where(row == b, keep_ref[b, c], keep)
        kept_ref[:, at] = jnp.where(keep > 0, 0.0, NEGATIVE)
    fresh_ref[pl.ds(0, ROWS), :] = jnp.where(row == mine, 0.0, NEGATIVE)
    seen = ((lane == 0) & (turn <= row)) | ((lane == 1) & (row == DRAFT) & (turn == 0))
    fresh_ref[pl.ds(ROWS, ROWS), :] = jnp.where(seen, 0.0, NEGATIVE)
    for load in loads[3:]:
        load.wait()
    rows = hidden_ref[...]
    query = jnp.dot(rows, query_ref[...], preferred_element_type=F32)
    for h in range(ROWS):
        flat[pl.ds(h, TOKENS, stride=ROWS), :] = query[:, h * LANES : (h + 1) * LANES]
    flat[pl.ds(QUERY_ROWS, TOKENS), :] = jnp.dot(rows, key_ref[...], preferred_element_type=F32)
    flat[pl.ds(QUERY_ROWS + TOKENS, TOKENS), :] = jnp.dot(
        rows, value_ref[...], preferred_element_type=F32
    )
    for d in range(SEQ):
        packed[pl.ds(d * MESSAGE + ROWS, ROWS), :] = jnp.zeros((ROWS, LANES), F32)
        packed[pl.ds(d * MESSAGE, QUERIES), :] = flat[pl.ds(d * QUERIES, QUERIES), :]
    for j in range(VERIFY):
        first = (j % OWNERS) * MESSAGE + QUERIES + 2 * (j // OWNERS)
        for k in range(2):
            packed[pl.ds(first + k, BATCH, stride=OWNERS * MESSAGE), :] = flat[
                pl.ds(QUERY_ROWS + k * TOKENS + j * BATCH, BATCH), :
            ]
    parts = packed[pl.ds(0, SEQ * MESSAGE), :]
    out_ref[...] = parts.reshape(SEQ, MESSAGE, LANES).astype(out_ref.dtype)


def rotate(parts_ref, cosine_ref, sine_ref, out_ref, own_ref):
    total = parts_ref[0].astype(F32)
    for s in range(1, SEQ):
        total += parts_ref[s].astype(F32)
    swapped = pltpu.roll(total, LANES // 2, 1)
    rotated = total * cosine_ref[...] + swapped * sine_ref[...]
    own_ref[...] = rotated[ROWS:]
    for k in range(QUERIES // 2):
        strip = rotated[2 * k : 2 * k + 2].astype(BF16)
        for s in range(SEQ):
            out_ref[s, :, k * LANES : (k + 1) * LANES] = strip


def split(value):
    high = value.astype(BF16).astype(F32)
    return high, (value - high).astype(BF16).astype(F32)


def attend(
    live_ref, kept_ref, fresh_ref, own_ref, spread_ref, keys, values,
    out_ref, scores, weights, results, tails, all_ref,
):
    blocks = keys.shape[1] // LANES
    lane = lax.broadcasted_iota(jnp.int32, (ROWS, LANES), 1)
    row = lax.broadcasted_iota(jnp.int32, (ROWS, LANES), 0)
    own = own_ref[...]
    first = QUERIES - ROWS
    new_keys, new_values = (
        jnp.concatenate(
            [
                jnp.where(
                    row == 0,
                    own[first + k : first + k + 1],
                    jnp.where(row == 1, own[first + k + 2 : first + k + 3], 0.0),
                ),
                jnp.zeros((LANES - ROWS, LANES), F32),
            ],
            axis=0,
        ).astype(BF16)
        for k in range(2)
    )
    for d in range(SEQ):
        for k in range(QUERIES // 2):
            strip = spread_ref[d, :, k * LANES : (k + 1) * LANES]
            all_ref[pl.ds(d * QUERIES + 2 * k, 2), :] = strip.astype(F32)
    transposed = (((1,), (1,)), ((), ()))
    exponent = SCALE * LOG2E

    def tile(j, b):
        return pl.ds((j * BATCH + b) * ROWS, ROWS)

    new_scores = (
        lax.dot_general(
            all_ref[...].astype(BF16), new_keys, transposed, preferred_element_type=F32
        )
        * exponent
    )
    for b in range(BATCH):
        query = jnp.concatenate([all_ref[tile(j, b), :] for j in range(VERIFY)], axis=0).astype(BF16)
        scores[b] = (
            lax.dot_general(query, keys[b], transposed, preferred_element_type=F32) * exponent
            + live_ref[b : b + 1, :]
        )
    kept, fresh, bases = [], [], []
    for b in range(BATCH):
        kept.append([kept_ref[b : b + 1, c * LANES : (c + 1) * LANES] for c in range(blocks)])
        rows = []
        for j in range(VERIFY):
            at = (j * BATCH + b) * ROWS
            bias = fresh_ref[b : b + 1, :] + fresh_ref[ROWS + j : ROWS + j + 1, :]
            rows.append(new_scores[at : at + ROWS] + bias)
        rows = jnp.concatenate(rows, axis=0)
        target, draft = rows, rows[: DRAFT * ROWS]
        fresh.append(jnp.concatenate([target, draft], axis=0))
        for c in range(blocks):
            block = scores[b, :, c * LANES : (c + 1) * LANES]
            target = jnp.maximum(target, block)
            draft = jnp.maximum(draft, block[: DRAFT * ROWS] + kept[b][c])
        peak = jnp.max(jnp.concatenate([target, draft], axis=0), axis=1, keepdims=True)
        bases.append(split(peak))
    totals, fresh_weights = [], []
    for b in range(BATCH):
        base = bases[b][0] + bases[b][1]
        base_target = base[: VERIFY * ROWS]
        base_draft = base[VERIFY * ROWS :]
        new_weights = jnp.exp2(fresh[b] - base)
        fresh_weights.append(new_weights)
        sums = new_weights
        for c in range(blocks):
            at = slice(c * LANES, (c + 1) * LANES)
            block = scores[b, :, at]
            result = jnp.concatenate(
                [
                    jnp.exp2(block - base_target),
                    jnp.exp2(block[: DRAFT * ROWS] + kept[b][c] - base_draft),
                ],
                axis=0,
            )
            sums += result
            weights[b, :, at] = result.astype(BF16)
        totals.append(jnp.sum(sums, axis=1, keepdims=True))
    fresh_result = jnp.dot(
        jnp.concatenate(fresh_weights, axis=0).astype(BF16),
        new_values,
        preferred_element_type=F32,
    )
    rows = TILES * ROWS
    packed = jnp.zeros((rows, LANES), F32)
    lanes = lax.broadcasted_iota(jnp.int32, (rows, LANES), 1)
    for b in range(BATCH):
        results[pl.ds(b * rows, rows), :] = (
            jnp.dot(weights[b], values[b], preferred_element_type=F32)
            + fresh_result[b * rows : (b + 1) * rows]
        )
        for k, value in enumerate(bases[b] + split(totals[b])):
            packed = jnp.where(lanes == k * BATCH + b, value, packed)
    stats = jnp.concatenate([packed, jnp.zeros((LANES - rows, LANES), F32)], axis=0).T
    for i in range(OWNERS):
        near = stats[: 4 * BATCH]
        if i:
            near = pltpu.roll(near, LANES - i * PAIRS, 1)
        far = pltpu.roll(near, LANES // 2, 1)
        for r in range(2):
            high = near[2 * r * BATCH : (2 * r + 1) * BATCH]
            low = far[(2 * r + 1) * BATCH : (2 * r + 2) * BATCH]
            every = pl.ds(i * SUB + 2 + r, BATCH, stride=OWNERS * SUB)
            tails[every, :] = jnp.where(lane < LANES // 2, high, low)
            tails[pl.ds(i * SUB + r, BATCH, stride=OWNERS * SUB), :] = results[
                pl.ds(i * PAIRS + 16 + r, BATCH, stride=rows), :
            ]
    for d in range(SEQ):
        for k in range(STRIPS):
            if k < STRIPS - 1:
                strip = results[pl.ds(d * PAIRS + k * SUB, SUB), :]
            else:
                strip = tails[pl.ds(d * SUB, SUB), :]
            out_ref[d, :, k * LANES : (k + 1) * LANES] = strip.astype(BF16)


def merge(parts_ref, out_ref, parts):
    for s in range(SEQ):
        for k in range(STRIPS):
            strip = parts_ref[s, :, k * LANES : (k + 1) * LANES]
            parts[pl.ds(s * SLOTS + k * SUB, SUB), :] = strip.astype(F32)
        parts[pl.ds(s * SLOTS + STRIPS * SUB, SUB), :] = jnp.zeros((SUB, LANES), F32)
    peaks = parts[pl.ds(PAIRS, SEQ, stride=SLOTS), :]
    peaks += pltpu.roll(peaks, LANES // 2, 1)
    totals = parts[pl.ds(PAIRS + 1, SEQ, stride=SLOTS), :]
    totals += pltpu.roll(totals, LANES // 2, 1)
    factors = jnp.exp2(peaks - jnp.max(peaks, axis=0, keepdims=True))
    total = jnp.sum(factors * totals, axis=0, keepdims=True)
    factors = factors / jnp.where(total > 0.0, total, 1.0)
    factors = jnp.concatenate([factors, jnp.zeros((LANES - SEQ, LANES), F32)], axis=0).T
    factors = factors[:SLOTS]
    merged = jnp.zeros((SLOTS, LANES), F32)
    for s in range(SEQ):
        merged += parts[pl.ds(s * SLOTS, SLOTS), :] * factors[:, s : s + 1]
    merged = merged.astype(BF16)
    for k in range(STRIPS):
        strip = merged[k * SUB : (k + 1) * SUB]
        for s in range(SEQ):
            out_ref[s, :, k * LANES : (k + 1) * LANES] = strip


def project_out(all_ref, weight_ref, out_ref, attended):
    for d in range(SEQ):
        for k in range(STRIPS):
            size = min(SUB, PAIRS - k * SUB)
            strip = all_ref[d, :, k * LANES : (k + 1) * LANES].astype(F32)
            attended[pl.ds(d * PAIRS + k * SUB, size), :] = strip[:size]
    total = None
    for h in range(ROWS):
        rows = jnp.concatenate(
            [attended[pl.ds(t * ROWS + h, BATCH, stride=TILES * ROWS), :] for t in range(TILES)],
            axis=0,
        ).astype(BF16)
        part = jnp.dot(
            rows, weight_ref[h * LANES : (h + 1) * LANES, :], preferred_element_type=F32
        )
        total = part if total is None else total + part
    out_ref[...] = total.astype(BF16)


def add_pair(mine_ref, other_ref, out_ref):
    rounded = (mine_ref[...].astype(F32) + other_ref[...].astype(F32)).astype(BF16)
    for x in range(CHIPS):
        out_ref[x] = rounded


def add_groups(parts_ref, verify_ref, draft_ref, *halves):
    summed = parts_ref[0].astype(F32)
    for h in range(1, CHIPS):
        summed += parts_ref[h].astype(F32)
    rounded = summed.astype(BF16)
    for j in range(VERIFY):
        verify_ref[j] = rounded[j * BATCH : (j + 1) * BATCH]
    for k, half in enumerate(halves):
        at = slice(k * LANES, (k + 1) * LANES)
        half[pl.ds(0, DRAFT * BATCH), :] = summed[TOKENS:, at]
        for b in range(BATCH):
            draft_ref[b, :, at] = half[pl.ds(b, DRAFT, stride=BATCH), :].astype(BF16)


VMEM = pl.BlockSpec(memory_space=pltpu.VMEM)
HBM = pl.BlockSpec(memory_space=pltpu.HBM)


def resident(array):
    return pltpu.with_memory_space_constraint(array, pltpu.VMEM)


def in_place(array):
    return pltpu.with_memory_space_constraint(array, pltpu.HBM)


def exchange(messages, axis):
    return lax.all_to_all(messages, axis, 0, 0, tiled=True)


def per_device(
    hidden_states,
    w_query,
    w_key,
    w_value,
    w_out,
    key_cache,
    value_cache,
    context_lengths,
    keep_blocks,
):
    width = hidden_states.shape[2]
    context = key_cache.shape[1]
    columns = w_out.shape[1]
    rows = hidden_states.transpose(1, 0, 2).reshape(TOKENS, width)
    half = LANES // 2
    inverse = (500000.0 ** (-(np.arange(LANES) % half) * 2.0 / LANES)).astype(np.float32)
    array = pltpu.VMEM
    parts, cosine, sine, live, kept, fresh = pl.pallas_call(
        project,
        out_shape=(
            array((SEQ, MESSAGE, LANES), BF16),
            array((MESSAGE, LANES), F32),
            array((MESSAGE, LANES), F32),
            array((BATCH, context), F32),
            array((BATCH, context), F32),
            array((2 * ROWS, LANES), F32),
        ),
        in_specs=[HBM] * 7,
        out_specs=(VMEM,) * 6,
        scratch_shapes=[
            pltpu.VMEM((TOKENS, width), BF16),
            pltpu.VMEM(w_query.shape, BF16),
            pltpu.VMEM(w_key.shape, BF16),
            pltpu.VMEM(w_value.shape, BF16),
            pltpu.SMEM(context_lengths.shape, jnp.int32),
            pltpu.SMEM(keep_blocks.shape, jnp.int32),
            pltpu.VMEM((1, LANES), F32),
            pltpu.VMEM((QUERY_ROWS + 2 * TOKENS, LANES), F32),
            pltpu.VMEM((SEQ * MESSAGE + SPARE, LANES), F32),
            pltpu.SemaphoreType.DMA((7,)),
        ],
        name="project",
        compiler_params=pltpu.CompilerParams(vmem_limit_bytes=8 << 20),
    )(
        *(
            in_place(operand)
            for operand in (
                rows, w_query, w_key, w_value, context_lengths, keep_blocks,
                jnp.asarray(inverse).reshape(1, LANES),
            )
        )
    )
    parts = exchange(parts, "seq")
    rotated, own = pl.pallas_call(
        rotate,
        out_shape=(
            pltpu.VMEM((SEQ, 2, QUERIES // 2 * LANES), BF16),
            pltpu.VMEM((ROWS, LANES), F32),
        ),
        in_specs=[VMEM] * 3,
        out_specs=(VMEM, VMEM),
        name="rotate",
        cost_estimate=pl.CostEstimate(
            flops=1000000000, transcendentals=0, bytes_accessed=64000000
        ),
        compiler_params=pltpu.CompilerParams(vmem_limit_bytes=8 << 20),
    )(resident(parts), resident(cosine), resident(sine))
    rotated = exchange(rotated, "seq")
    partial = pl.pallas_call(
        attend,
        out_shape=pltpu.VMEM((SEQ, SUB, STRIPS * LANES), BF16),
        in_specs=[VMEM] * 7,
        out_specs=VMEM,
        scratch_shapes=[
            pltpu.VMEM((BATCH, VERIFY * ROWS, context), F32),
            pltpu.VMEM((BATCH, TILES * ROWS, context), BF16),
            pltpu.VMEM((BATCH * TILES * ROWS + SPARE, LANES), F32),
            pltpu.VMEM((SEQ * SUB + SPARE, LANES), F32),
            pltpu.VMEM((QUERY_ROWS, LANES), F32),
        ],
        name="attend",
        compiler_params=pltpu.CompilerParams(vmem_limit_bytes=16 << 20),
    )(
        resident(live),
        resident(kept),
        resident(fresh),
        resident(own),
        resident(rotated),
        resident(key_cache),
        resident(value_cache),
    )
    partial = exchange(partial, "seq")
    merged = pl.pallas_call(
        merge,
        out_shape=pltpu.VMEM((SEQ, SUB, STRIPS * LANES), BF16),
        in_specs=[VMEM],
        out_specs=VMEM,
        scratch_shapes=[pltpu.VMEM((SEQ * SLOTS + SPARE, LANES), F32)],
        name="merge",
        compiler_params=pltpu.CompilerParams(vmem_limit_bytes=8 << 20),
    )(resident(partial))
    merged = exchange(merged, "seq")
    groups = pl.pallas_call(
        project_out,
        out_shape=pltpu.VMEM((BATCH * TILES, columns), BF16),
        in_specs=[VMEM, VMEM],
        out_specs=VMEM,
        scratch_shapes=[pltpu.VMEM((BATCH * TILES * ROWS + SPARE, LANES), F32)],
        name="project_out",
        compiler_params=pltpu.CompilerParams(vmem_limit_bytes=8 << 20),
    )(resident(merged), resident(w_out))
    other = lax.ppermute(groups, "head", [(h, h ^ 1) for h in range(HEADS)])
    pairs = pl.pallas_call(
        add_pair,
        out_shape=pltpu.VMEM((CHIPS, BATCH * TILES, columns), BF16),
        in_specs=[VMEM, VMEM],
        out_specs=VMEM,
        name="add_pair",
        compiler_params=pltpu.CompilerParams(vmem_limit_bytes=8 << 20),
    )(resident(groups), resident(other))
    across = [[x * CORES + c for x in range(CHIPS)] for c in range(CORES)]
    pairs = lax.all_to_all(pairs, "head", 0, 0, tiled=True, axis_index_groups=across)
    verify_out, draft_out = pl.pallas_call(
        add_groups,
        out_shape=(
            jax.ShapeDtypeStruct((VERIFY, BATCH, columns), BF16),
            jax.ShapeDtypeStruct((BATCH, DRAFT, columns), BF16),
        ),
        in_specs=[VMEM],
        out_specs=(VMEM, VMEM),
        scratch_shapes=[pltpu.VMEM((DRAFT * BATCH + SPARE, LANES), F32)] * (columns // LANES),
        name="add_groups",
        compiler_params=pltpu.CompilerParams(vmem_limit_bytes=8 << 20),
    )(resident(pairs))
    return verify_out.transpose(1, 0, 2), draft_out


def solution(mesh):
    placed = (
        P(None, None, "seq"),
        P("seq", "head"),
        P("seq", "head"),
        P("seq", "head"),
        P("head", "seq"),
        P(None, "seq", "head"),
        P(None, "seq", "head"),
        P(),
        P(None, "seq"),
    )
    return jax.shard_map(
        per_device,
        mesh=mesh,
        in_specs=placed,
        out_specs=(P(None, None, "seq"), P(None, None, "seq")),
        check_vma=False,
    )
```
